128 devices in a mesh: row: 16 (over y_hi, z, core), col: 8 (over x, y_lo).
Axes of the slice: x: 4, y: 4 (y_hi: 2, y_lo: 2; y = y_hi * 2 + y_lo), z: 4, core: 2. Of those that a mesh axis runs over, the one named last changes fastest.
Arguments:
- cells: float32 [4096, 1024], P(('row', 'col')), may hold values from 0 to 1
- instance_cell: int32 [64, 256], P('row', 'col'), may hold values from 0 to 4095, as said below
- target: float32 [2048, 8192], P('row', 'col'), may hold values from 0 to 1
- row_taps: float32 [8, 65], replicated, may hold values from -0.75 to 0.75
- col_taps: float32 [8, 65], replicated, may hold values from -0.75 to 0.75
- kernel_weight: float32 [8], replicated, may hold values from 0.05 to 0.5
Outputs:
- cells_out: float32 [4096, 1024], P(('row', 'col'))
The draws below stay inside these ranges and needn't reach their ends.
Inputs may be any that keep to these rules, and one draw needn't show every extreme that they name: `instance_cell`: each entry is the index of the device that holds the cell, along row+col with row slowest, times 32, plus the cell's place there. Tile (a, b) lies on device (a // 4, b // 32). Among one device's tiles at most 2 name cells held by any one device, and one holding device is named by exactly 2 tiles of every device.
All inputs are finite; a program needn't handle non-finite values.
Results may differ from the reference program's by a relative error of at most 0.00016.
Values sent between devices are 32-bit elements; how exact they have to be, the bound alone decides.
A program may use at most 128 MiB of HBM per device.

```python
import math
import jax
import jax.numpy as jnp
from jax import lax

TILE = 32
TAPS = 65
HALF = 32
KERNELS = 8
ITERS = 1
CR = 128
CC = 1024
SLOTS = 32
OWNERS = 128
NR = 2048
NC = 8192
TPD = 128
CAP = 2
CELLS = 4096


def draw_instance_cell(key, part):
    owners = OWNERS
    tiles_here = TPD
    hottest = jax.random.randint(jax.random.fold_in(key, 7), (), 0, owners)

    def one_device(device):
        subkey = jax.random.fold_in(key, device + 11)
        others = (hottest + 1 + jax.random.permutation(jax.random.fold_in(subkey, 1), owners - 1)) % owners
        placing = jnp.arange(tiles_here)
        rest_index = jnp.maximum(placing - CAP, 0) % (owners - 1)
        owner_index = jnp.where(placing < CAP, hottest, others[rest_index])
        owner_index = jax.random.permutation(jax.random.fold_in(subkey, 2), owner_index)
        slot_index = jax.random.randint(jax.random.fold_in(subkey, 3), (tiles_here,), 0, SLOTS)
        return owner_index * SLOTS + slot_index
    table = jax.vmap(one_device)(jnp.arange(owners))
    row_count = NR // CR
    col_count = NC // CC
    table = table.reshape(row_count, col_count, CR // TILE, CC // TILE).transpose(0, 2, 1, 3)
    return table.reshape(row_count * (CR // TILE), col_count * (CC // TILE)).astype(jnp.int32)


def level_of(rng, shape, split, least, largest):
    factor_of = 1.0
    for dim, shards_of in split:
        steps = jax.random.uniform(jax.random.fold_in(jax.random.fold_in(rng, 6), dim), (shards_of,), jnp.float32, least / len(split), largest / len(split))
        factor_of = factor_of * jnp.repeat(jnp.exp(steps), shape[dim] // shards_of).reshape((-1,) + (1,) * (len(shape) - 1 - dim))
    return factor_of


def bell_draw(rng, extent, scale, bound, kind=jnp.bfloat16):
    array = scale * jax.random.normal(rng, extent, jnp.float32)
    return jnp.clip(array, min=-bound, max=bound).astype(kind)


def setup_inputs(seed: int = 0) -> dict:
    arg_keys = jax.random.split(jax.random.key(seed), 7)
    cells = jnp.clip(1.0 * jax.random.uniform(arg_keys[0], (CELLS, TILE * TILE), jnp.float32) ** level_of(arg_keys[0], (CELLS, TILE * TILE), ((0, 128),), -0.2, 0.2), 0.0, 1.0)
    instance_cell = draw_instance_cell(jax.random.fold_in(arg_keys[6], 71), 0)
    target = jnp.clip(1.0 * jax.random.uniform(arg_keys[2], (NR, NC), jnp.float32) ** level_of(arg_keys[2], (NR, NC), ((0, 16), (1, 8)), -0.2, 0.2), 0.0, 1.0)
    row_taps = bell_draw(arg_keys[3], (KERNELS, TAPS), TAPS ** -0.5, 0.75, jnp.float32)
    col_taps = bell_draw(arg_keys[4], (KERNELS, TAPS), TAPS ** -0.5, 0.75, jnp.float32)
    kernel_weight = jnp.clip(jnp.exp(jax.random.uniform(arg_keys[5], (KERNELS,), jnp.float32, math.log(0.05), math.log(0.5))), 0.05, 0.5)
    return {"cells": cells, "instance_cell": instance_cell, "target": target, "row_taps": row_taps, "col_taps": col_taps, "kernel_weight": kernel_weight}


STEEPNESS = 4.0
THRESHOLD = 0.3
STEP_RATE = 0.5
HIGHEST = lax.Precision.HIGHEST


def toeplitz_bands(taps):
    kernels = taps.shape[0]
    front = jnp.zeros((kernels, 127), jnp.float32)
    back = jnp.zeros((kernels, 256), jnp.float32)
    padded = jnp.concatenate([front, taps.astype(jnp.float32), back], axis=1)
    length = padded.shape[1]
    repeated = jnp.tile(padded, (1, 128))[:, : 128 * (length - 1)]
    shaped = repeated.reshape(kernels, 128, length - 1)[:, :, 127:383]
    return shaped.transpose(0, 2, 1)


def along_last(values, band):
    breadth = values.shape[-1] - (TAPS - 1)
    blocks = -(-breadth // 128)
    padding = blocks * 128 + 128 - values.shape[-1]
    lead_shape = values.shape[:-1]
    padded = jnp.pad(values, [(0, 0)] * len(lead_shape) + [(0, padding)])
    leading = padded[..., : blocks * 128].reshape(lead_shape + (blocks, 128))
    trailing = padded[..., 128:].reshape(lead_shape + (blocks, 128))
    result = jnp.einsum("...nb,bm->...nm", leading, band[:128], precision=HIGHEST)
    result = result + jnp.einsum("...nb,bm->...nm", trailing, band[128:], precision=HIGHEST)
    return result.reshape(lead_shape + (blocks * 128,))[..., :breadth]


def along_first(values, band):
    height = values.shape[0] - (TAPS - 1)
    blocks = -(-height // 128)
    padding = blocks * 128 + 128 - values.shape[0]
    columns = values.shape[1]
    padded = jnp.pad(values, [(0, padding), (0, 0)])
    leading = padded[: blocks * 128].reshape(blocks, 128, columns)
    trailing = padded[128:].reshape(blocks, 128, columns)
    result = jnp.einsum("nbc,bm->nmc", leading, band[:128], precision=HIGHEST)
    result = result + jnp.einsum("nbc,bm->nmc", trailing, band[128:], precision=HIGHEST)
    return result.reshape(blocks * 128, columns)[:height]


def image_field(widened, row_band, col_band):
    return along_first(along_last(widened, col_band), row_band)


def reference(cells, instance_cell, target, row_taps, col_taps, kernel_weight):
    row_bands = toeplitz_bands(row_taps)
    col_bands = toeplitz_bands(col_taps)
    row_flips = toeplitz_bands(row_taps[:, ::-1])
    col_flips = toeplitz_bands(col_taps[:, ::-1])
    tile_rows, tile_cols = instance_cell.shape
    flat_cells = instance_cell.reshape(-1).astype(jnp.int32)
    current = cells
    for iteration in range(ITERS):
        tiles = jnp.take(current, flat_cells, axis=0)
        mask = tiles.reshape(tile_rows, tile_cols, TILE, TILE).transpose(0, 2, 1, 3).reshape(tile_rows * TILE, tile_cols * TILE)
        widened = jnp.pad(mask, HALF)

        def forward_kernel(total, pieces):
            row_band, col_band, weight = pieces
            field = image_field(widened, row_band, col_band)
            return total + weight * field * field, None

        intensity, unused = lax.scan(forward_kernel, jnp.zeros_like(mask), (row_bands, col_bands, kernel_weight))
        resist = jax.nn.sigmoid(STEEPNESS * (intensity - THRESHOLD))
        sensitivity = 2.0 * (resist - target) * STEEPNESS * resist * (1.0 - resist)

        def adjoint_kernel(total, pieces):
            row_band, col_band, row_flip, col_flip, weight = pieces
            field = image_field(widened, row_band, col_band)
            spread = jnp.pad(2.0 * weight * sensitivity * field, HALF)
            return total + image_field(spread, row_flip, col_flip), None

        gradient, unused = lax.scan(adjoint_kernel, jnp.zeros_like(mask), (row_bands, col_bands, row_flips, col_flips, kernel_weight))
        tile_grads = gradient.reshape(tile_rows, TILE, tile_cols, TILE).transpose(0, 2, 1, 3).reshape(-1, TILE * TILE)
        summed = jax.ops.segment_sum(tile_grads, flat_cells, num_segments=current.shape[0])
        current = current - STEP_RATE * summed
    return current
```

```python
import functools

import jax
import jax.numpy as jnp
from jax import lax
from jax.experimental import pallas as pl
from jax.experimental.pallas import tpu as pltpu
from jax.sharding import PartitionSpec as P

TILE = 32
TAPS = 65
KERNELS = 8
ROWS = 128
COLS = 1024
TILE_ROWS = 4
TILE_COLS = 32
TILES = 128
SLOTS = 32
WIDE = 36
GROUPS = 9
STEEPNESS = 4.0
THRESHOLD = 0.3
STEP_RATE = 0.5
MESH = pl.DeviceIdType.MESH
BF16 = jnp.bfloat16
F32 = jnp.float32
I32 = jnp.int32
WHOLE = pl.BlockSpec(memory_space=pltpu.VMEM)
SCALARS = pl.BlockSpec(memory_space=pltpu.SMEM)

NEIGHBOURS = tuple((dr, dc) for dr in (-1, 0, 1) for dc in (-1, 0, 1) if (dr, dc) != (0, 0))


def span(step, count, inside):
    if step == 0:
        return pl.ds(1, count)
    if step < 0:
        return pl.ds(1 if inside else 0, 1)
    return pl.ds(count if inside else count + 1, 1)


def split(value):
    high = value.astype(BF16)
    return high, (value - high.astype(F32)).astype(BF16)


def mm(a, b):
    return jnp.dot(a, b, preferred_element_type=F32)


def swap_blocks(vectors):
    lane = lax.broadcasted_iota(I32, vectors[0].shape, 2)
    low = lane < 64
    even = (lane & 32) == 0
    a, b, c, d = vectors
    a, c = (
        jnp.where(low, a, pltpu.roll(c, 64, 2)),
        jnp.where(low, pltpu.roll(a, 64, 2), c),
    )
    b, d = (
        jnp.where(low, b, pltpu.roll(d, 64, 2)),
        jnp.where(low, pltpu.roll(b, 64, 2), d),
    )
    a, b = (
        jnp.where(even, a, pltpu.roll(b, 32, 2)),
        jnp.where(even, pltpu.roll(a, 96, 2), b),
    )
    c, d = (
        jnp.where(even, c, pltpu.roll(d, 32, 2)),
        jnp.where(even, pltpu.roll(c, 96, 2), d),
    )
    return a, b, c, d


def bands_kernel(row_taps, col_taps, a_hi, a_lo, at_hi, at_lo, b_both, bt_both, pad):
    pad[...] = jnp.zeros_like(pad)
    pad[0:8, 0:TAPS] = row_taps[...]
    pad[8:16, 0:TAPS] = col_taps[...]
    c = lax.broadcasted_iota(I32, (256, 256), 0)
    p = lax.broadcasted_iota(I32, (256, 256), 1)
    placed = (c & ~31) + ((c & 3) << 3) + ((c & 31) >> 2)
    permute = (p == placed).astype(F32).astype(BF16)

    def shifted(line):
        row = pad[pl.ds(line, 1), :]
        return pltpu.roll(jnp.broadcast_to(row, (128, 256)), 0, 1, stride=1, stride_axis=0)

    for k in range(KERNELS):
        rows = pl.ds(k * 128, 128)
        for part, a_out, at_out in zip(split(shifted(k)), (a_hi, a_lo), (at_hi, at_lo)):
            ordered = mm(part, permute)
            a_out[rows, :] = ordered.astype(BF16)
            at_out[:, rows] = ordered.T.astype(BF16)
        for i, part in enumerate(split(shifted(8 + k))):
            part = part.astype(F32)
            lanes = pl.ds(i * 128, 128)
            b_both[k, :, lanes] = part.T.astype(BF16)
            bt_both[k, 0:128, lanes] = part[:, 128:256].astype(BF16)
            bt_both[k, 128:256, lanes] = part[:, 0:128].astype(BF16)


def image_kernel(
    weight, wide, target, a_hi, a_lo, at_hi, at_lo, b_both, bt_both, out,
    x_hi, x_lo, y_hi, y_lo, fields, p_hi, p_lo, q_hi, q_lo,
):
    x_hi[192:256, :] = jnp.zeros((64, GROUPS * 128), BF16)
    x_lo[192:256, :] = jnp.zeros((64, GROUPS * 128), BF16)
    for g in range(GROUPS):
        turned = swap_blocks([wide[:, 4 * g + q] for q in range(4)])
        value = jnp.concatenate(turned, axis=1).reshape(192, 128)
        lanes = pl.ds(g * 128, 128)
        x_hi[0:192, lanes], x_lo[0:192, lanes] = split(value)
    for g in range(GROUPS):
        lanes = pl.ds(g * 128, 128)
        high, low = x_hi[:, lanes], x_lo[:, lanes]
        both = mm(a_hi[...], jnp.concatenate([high, low], axis=1))
        value = both[:, :128] + both[:, 128:] + mm(a_lo[...], high)
        y_hi[:, g], y_lo[:, g] = (v.reshape(KERNELS, 128, 128) for v in split(value))
    intensity = jnp.zeros((1024, 128), F32)
    for k in range(KERNELS):
        def window(ref):
            return jnp.concatenate(
                [ref[k, 0:8].reshape(1024, 128), ref[k, 1:9].reshape(1024, 128)], axis=1
            )
        both = mm(window(y_hi), b_both[k])
        field = both[:, :128] + both[:, 128:] + mm(window(y_lo), b_both[k, :, 0:128])
        fields[k] = field
        intensity = intensity + weight[k] * field * field
    wanted = jnp.concatenate([target[:, 128 * n:128 * n + 128] for n in range(8)], axis=0)
    resist = 1.0 / (1.0 + jnp.exp(-STEEPNESS * (intensity - THRESHOLD)))
    sensitivity = 2.0 * (resist - wanted) * STEEPNESS * resist * (1.0 - resist)
    for ref in (p_hi, p_lo):
        ref[0] = jnp.zeros((128, 128), BF16)
        ref[9] = jnp.zeros((128, 128), BF16)
    for k in range(KERNELS):
        product = (2.0 * weight[k]) * sensitivity * fields[k]
        p_hi[1:9], p_lo[1:9] = (v.reshape(8, 128, 128) for v in split(product))

        def window(ref):
            return jnp.concatenate(
                [ref[0:9].reshape(1152, 128), ref[1:10].reshape(1152, 128)], axis=1
            )
        both = mm(window(p_hi), bt_both[k])
        value = both[:, :128] + both[:, 128:] + mm(window(p_lo), bt_both[k, :, 0:128])
        high, low = split(value)
        for g in range(GROUPS):
            lanes = pl.ds(g * 128, 128)
            rows = pl.ds(k * 128, 128)
            q_hi[rows, lanes] = high[128 * g:128 * g + 128]
            q_lo[rows, lanes] = low[128 * g:128 * g + 128]
    for g in range(GROUPS):
        lanes = pl.ds(g * 128, 128)
        high, low = q_hi[:, lanes], q_lo[:, lanes]
        both = mm(at_hi[0:192, :], jnp.concatenate([high, low], axis=1))
        value = both[:, :128] + both[:, 128:] + mm(at_lo[0:192, :], high)
        value = value.reshape(6, 32, 128)
        turned = swap_blocks([value[:, 8 * s:8 * s + 8] for s in range(4)])
        for q in range(4):
            out[:, 4 * g + q] = turned[q]


def place(mesh_shape):
    row_count, col_count = mesh_shape
    row, col = lax.axis_index("row"), lax.axis_index("col")
    return row_count, col_count, row, col, row * col_count + col


def everyone(total, col_count, me, body):
    def step(i, carry):
        peer = lax.rem(me + i, total)
        body(peer, (peer // col_count, lax.rem(peer, col_count)))
        return carry
    lax.fori_loop(1, total, step, 0)


def greet_all(total, col_count, me):
    barrier = pltpu.get_barrier_semaphore()

    def signal(peer, where):
        pl.semaphore_signal(barrier, inc=1, device_id=where, device_id_type=MESH)
    everyone(total, col_count, me, signal)
    return barrier


def exists(coords, counts):
    ok = None
    for at, count, step in coords:
        if step == 0:
            continue
        here = (at + step >= 0) if step < 0 else (at + step < count)
        ok = here if ok is None else jnp.logical_and(ok, here)
    return ok


def fetch_kernel(
    mesh_shape, inst, cells, wide, tile_of, selected,
    pad, mine, table, cells3, outgoing, arrived, index_v, index_s, where_v, where_s,
    table_send, table_recv, cell_send, cell_recv, halo_send, halo_recv, local,
):
    row_count, col_count, row, col, me = place(mesh_shape)
    total = row_count * col_count
    for a in (0, 5):
        wide[a] = jnp.zeros((WIDE, 8, 128), F32)
    for b in (0, 33, 34, 35):
        wide[1:5, b] = jnp.zeros((TILE_ROWS, 8, 128), F32)
    barrier = greet_all(total, col_count, me)
    pad[...] = jnp.zeros_like(pad)
    pad[0:TILE_ROWS, 0:TILE_COLS] = inst[...]
    lines = pad[...]
    line = lax.broadcasted_iota(I32, lines.shape, 0)
    flat = jnp.zeros((8, 128), I32)
    for a in range(TILE_ROWS):
        moved = pltpu.roll(lines, 32 * a, 1) if a else lines
        flat = flat + jnp.where(line == a, moved, 0)
    flat = jnp.sum(flat, axis=0, keepdims=True)
    mine[0] = flat
    table[me] = flat
    for r in range(8):
        cells3[:, r, :] = cells[:, 128 * r:128 * r + 128]
    pl.semaphore_wait(barrier, total - 1)

    def send_table(peer, where):
        pltpu.make_async_remote_copy(
            src_ref=mine, dst_ref=table.at[pl.ds(me, 1)], send_sem=table_send, recv_sem=table_recv,
            device_id=where, device_id_type=MESH,
        ).start()
    everyone(total, col_count, me, send_table)

    lane = lax.broadcasted_iota(I32, (128, 128), 1)
    sub = lax.broadcasted_iota(I32, (128, 128), 0)
    diagonal = lane == sub

    def as_row(column):
        return jnp.sum(jnp.where(diagonal, column, 0), axis=0, keepdims=True)
    owner = flat >> 5
    held = owner == sub
    first = jnp.min(jnp.where(held, lane, TILES), axis=1, keepdims=True)
    last = jnp.max(jnp.where(held, lane, -1), axis=1, keepdims=True)
    second = jnp.sum(jnp.where(held & (lane != first), 1, 0), axis=0, keepdims=True)
    tile_of[0:1, :] = as_row(jnp.minimum(first, TILES - 1))
    tile_of[1:2, :] = as_row(jnp.maximum(last, 0))
    where_v[...] = owner * 2 + second
    where_copy = pltpu.make_async_copy(where_v, where_s, local.at[0])
    where_copy.start()

    others = pl.ds(0, total - 1)
    neighbour = (lax.rem(row + 1, row_count), col)
    arrival = pltpu.make_async_remote_copy(
        src_ref=table.at[others], dst_ref=table.at[others], send_sem=table_send, recv_sem=table_recv,
        device_id=neighbour, device_id_type=MESH,
    )
    arrival.wait()

    asked = table[...].reshape(128, 128)
    hit = (asked >> 5) == me
    key = lane * SLOTS + (asked & (SLOTS - 1))
    first = jnp.min(jnp.where(hit, key, TILES * SLOTS), axis=1, keepdims=True)
    last = jnp.max(jnp.where(hit, key, -1), axis=1, keepdims=True)
    chosen = (
        as_row(jnp.where(first < TILES * SLOTS, first & (SLOTS - 1), -1)),
        as_row(jnp.where(last > first, last & (SLOTS - 1), -1)),
    )
    for s in range(2):
        selected[s:s + 1, :] = chosen[s]
        index_v[s:s + 1, :] = jnp.maximum(chosen[s], 0)
    index_copy = pltpu.make_async_copy(index_v, index_s, local.at[1])
    index_copy.start()
    index_copy.wait()

    def send_cells(peer, where):
        for s in range(2):
            outgoing[2 * peer + s] = cells3[index_s[s, peer]]
        pltpu.make_async_remote_copy(
            src_ref=outgoing.at[pl.ds(2 * peer, 2)], dst_ref=arrived.at[pl.ds(2 * me, 2)],
            send_sem=cell_send, recv_sem=cell_recv, device_id=where, device_id_type=MESH,
        ).start()
    everyone(total, col_count, me, send_cells)
    for s in range(2):
        arrived[2 * me + s] = cells3[index_s[s, me]]
    where_copy.wait()
    others = pl.ds(0, 2 * (total - 1))
    pltpu.make_async_remote_copy(
        src_ref=outgoing.at[others], dst_ref=arrived.at[others], send_sem=cell_send, recv_sem=cell_recv,
        device_id=neighbour, device_id_type=MESH,
    ).wait()

    def put(t, carry):
        wide[1 + t // TILE_COLS, 1 + lax.rem(t, TILE_COLS)] = arrived[where_s[0, t]]
        return carry
    lax.fori_loop(0, TILES, put, 0)

    def halo(i, dr, dc):
        return pltpu.make_async_remote_copy(
            src_ref=wide.at[span(dr, TILE_ROWS, True), span(dc, TILE_COLS, True)],
            dst_ref=wide.at[span(-dr, TILE_ROWS, False), span(-dc, TILE_COLS, False)],
            send_sem=halo_send.at[i], recv_sem=halo_recv.at[i],
            device_id=(row + dr, col + dc), device_id_type=MESH,
        )
    exchange(halo, row_count, col_count, row, col)


def exchange(halo, row_count, col_count, row, col):
    for i, (dr, dc) in enumerate(NEIGHBOURS):
        @pl.when(exists(((row, row_count, dr), (col, col_count, dc)), None))
        def _():
            halo(i, dr, dc).start()
    for i, (dr, dc) in enumerate(NEIGHBOURS):
        @pl.when(exists(((row, row_count, dr), (col, col_count, dc)), None))
        def _():
            halo(i, dr, dc).wait_send()

        @pl.when(exists(((row, row_count, -dr), (col, col_count, -dc)), None))
        def _():
            halo(i, dr, dc).wait_recv()


def return_kernel(
    mesh_shape, tile_of, grad, selected, cells, out,
    halo_row, halo_col, halo_corner, own, outgoing, back,
    send, recv, halo_send, halo_recv,
):
    row_count, col_count, row, col, me = place(mesh_shape)
    total = row_count * col_count
    for ref in (halo_row, halo_col, halo_corner):
        ref[...] = jnp.zeros_like(ref)
    barrier = greet_all(total, col_count, me)
    own[...] = grad[1:5, 1:33].reshape(TILES, 8, 128)
    pl.semaphore_wait(barrier, total - 1)

    def halo(i, dr, dc):
        if dr == 0:
            source = grad.at[pl.ds(1, TILE_ROWS), 0 if dc < 0 else TILE_COLS + 1]
            target = halo_col.at[0 if dc < 0 else 1]
        elif dc == 0:
            source = grad.at[0 if dr < 0 else TILE_ROWS + 1, pl.ds(1, TILE_COLS)]
            target = halo_row.at[0 if dr < 0 else 1]
        else:
            source = grad.at[0 if dr < 0 else TILE_ROWS + 1, 0 if dc < 0 else TILE_COLS + 1]
            target = halo_corner.at[2 * (dr > 0) + (dc > 0)]
        return pltpu.make_async_remote_copy(
            src_ref=source, dst_ref=target, send_sem=halo_send.at[i], recv_sem=halo_recv.at[i],
            device_id=(row + dr, col + dc), device_id_type=MESH,
        )
    exchange(halo, row_count, col_count, row, col)
    own[96:128] = own[96:128] + halo_row[0]
    own[0:32] = own[0:32] + halo_row[1]
    for a in range(TILE_ROWS):
        t = TILE_COLS * a
        own[t + 31] = own[t + 31] + halo_col[0, a]
        own[t] = own[t] + halo_col[1, a]
    for i, t in enumerate((127, 96, 31, 0)):
        own[t] = own[t] + halo_corner[i]

    def send_grads(peer, where):
        for s in range(2):
            outgoing[2 * peer + s] = own[tile_of[s, peer]]
        pltpu.make_async_remote_copy(
            src_ref=outgoing.at[pl.ds(2 * peer, 2)], dst_ref=back.at[pl.ds(2 * me, 2)],
            send_sem=send, recv_sem=recv, device_id=where, device_id_type=MESH,
        ).start()
    everyone(total, col_count, me, send_grads)
    for s in range(2):
        back[2 * me + s] = own[tile_of[s, me]]
    cell = lax.broadcasted_iota(I32, (SLOTS, 128), 0)
    selector = jnp.concatenate(
        [(cell == selected[s:s + 1, :]).astype(F32).astype(BF16) for s in range(2)], axis=1
    )
    others = pl.ds(0, 2 * (total - 1))
    pltpu.make_async_remote_copy(
        src_ref=outgoing.at[others], dst_ref=back.at[others], send_sem=send, recv_sem=recv,
        device_id=(lax.rem(row + 1, row_count), col), device_id_type=MESH,
    ).wait()
    flat = back.reshape(2 * TILES * 8, 128)
    for r in range(8):
        value = jnp.concatenate(
            [flat[pl.ds(8 * s + r, 128, stride=16), :] for s in range(2)], axis=0
        )
        high, low = split(value)
        tail = (value - high.astype(F32) - low.astype(F32)).astype(BF16)
        parts = mm(selector, jnp.concatenate([high, low, tail], axis=1))
        total_r = parts[:, 0:128] + parts[:, 128:256] + parts[:, 256:384]
        lanes = slice(128 * r, 128 * r + 128)
        out[:, lanes] = cells[:, lanes] - STEP_RATE * total_r


def shards(mesh_shape, cells, instance_cell, target, row_taps, col_taps, kernel_weight):
    sds = jax.ShapeDtypeStruct
    vmem = pltpu.VMEM
    dma = pltpu.SemaphoreType.DMA
    bands = pl.pallas_call(
        bands_kernel,
        name="bands",
        out_shape=(
            sds((1024, 256), BF16), sds((1024, 256), BF16),
            sds((256, 1024), BF16), sds((256, 1024), BF16),
            sds((8, 256, 256), BF16), sds((8, 256, 256), BF16),
        ),
        in_specs=[WHOLE] * 2,
        out_specs=(WHOLE,) * 6,
        scratch_shapes=[vmem((16, 256), F32)],
    )(row_taps, col_taps)
    wide, tile_of, selected = pl.pallas_call(
        functools.partial(fetch_kernel, mesh_shape),
        name="fetch",
        out_shape=(sds((6, WIDE, 8, 128), F32), sds((2, 128), I32), sds((2, 128), I32)),
        in_specs=[WHOLE] * 2,
        out_specs=(WHOLE,) * 3,
        scratch_shapes=[
            vmem((8, 128), I32), vmem((1, 1, 128), I32), vmem((128, 1, 128), I32),
            vmem((SLOTS, 8, 128), F32), vmem((256, 8, 128), F32), vmem((256, 8, 128), F32),
            vmem((2, 128), I32), pltpu.SMEM((2, 128), I32), vmem((1, 128), I32), pltpu.SMEM((1, 128), I32),
            dma, dma, dma, dma, dma((8,)), dma((8,)), dma((2,)),
        ],
        compiler_params=pltpu.CompilerParams(collective_id=0, has_side_effects=True),
    )(instance_cell, cells)
    grad = pl.pallas_call(
        image_kernel,
        name="image",
        out_shape=sds((6, WIDE, 8, 128), F32),
        in_specs=[SCALARS] + [WHOLE] * 8,
        out_specs=WHOLE,
        scratch_shapes=[
            vmem((256, 1152), BF16), vmem((256, 1152), BF16),
            vmem((8, 9, 128, 128), BF16), vmem((8, 9, 128, 128), BF16),
            vmem((8, 1024, 128), F32),
            vmem((10, 128, 128), BF16), vmem((10, 128, 128), BF16),
            vmem((1024, 1152), BF16), vmem((1024, 1152), BF16),
        ],
    )(kernel_weight, wide, target, *bands)
    return pl.pallas_call(
        functools.partial(return_kernel, mesh_shape),
        name="give",
        out_shape=sds((SLOTS, 1024), F32),
        in_specs=[SCALARS] + [WHOLE] * 3,
        out_specs=WHOLE,
        scratch_shapes=[
            vmem((2, 32, 8, 128), F32), vmem((2, 4, 8, 128), F32), vmem((4, 8, 128), F32),
            vmem((TILES, 8, 128), F32), vmem((256, 8, 128), F32), vmem((256, 8, 128), F32),
            dma, dma, dma((8,)), dma((8,)),
        ],
        compiler_params=pltpu.CompilerParams(collective_id=1, has_side_effects=True),
    )(tile_of, grad, selected, cells)


def solution(mesh):
    placed = (P(("row", "col"), None), P("row", "col"), P("row", "col"), P(), P(), P())
    return jax.shard_map(
        functools.partial(shards, (mesh.shape["row"], mesh.shape["col"])),
        mesh=mesh, in_specs=placed, out_specs=P(("row", "col"), None), check_vma=False,
    )
```

```python
import functools
import itertools

import jax
import jax.numpy as jnp
from jax import lax
from jax.experimental import pallas as pl
from jax.experimental.pallas import tpu as pltpu
from jax.sharding import PartitionSpec as P

TILE = 32
TAPS = 65
KERNELS = 8
ROWS = 128
COLS = 1024
TILE_ROWS = 4
TILE_COLS = 32
TILES = 128
SLOTS = 32
WIDE = 36
GROUPS = 9
STEEPNESS = 4.0
THRESHOLD = 0.3
STEP_RATE = 0.5
MESH = pl.DeviceIdType.MESH
BF16 = jnp.bfloat16
F32 = jnp.float32
I32 = jnp.int32
WHOLE = pl.BlockSpec(memory_space=pltpu.VMEM)
SCALARS = pl.BlockSpec(memory_space=pltpu.SMEM)

NEIGHBOURS = tuple((dr, dc) for dr in (-1, 0, 1) for dc in (-1, 0, 1) if (dr, dc) != (0, 0))


def span(step, count, inside):
    if step == 0:
        return pl.ds(1, count)
    if step < 0:
        return pl.ds(1 if inside else 0, 1)
    return pl.ds(count if inside else count + 1, 1)


def split(value):
    high = value.astype(BF16)
    return high, (value - high.astype(F32)).astype(BF16)


def mm(a, b):
    return jnp.dot(a, b, preferred_element_type=F32)


def swap_blocks(vectors):
    lane = lax.broadcasted_iota(I32, vectors[0].shape, 2)
    low = lane < 64
    even = (lane & 32) == 0
    a, b, c, d = vectors
    a, c = (
        jnp.where(low, a, pltpu.roll(c, 64, 2)),
        jnp.where(low, pltpu.roll(a, 64, 2), c),
    )
    b, d = (
        jnp.where(low, b, pltpu.roll(d, 64, 2)),
        jnp.where(low, pltpu.roll(b, 64, 2), d),
    )
    a, b = (
        jnp.where(even, a, pltpu.roll(b, 32, 2)),
        jnp.where(even, pltpu.roll(a, 96, 2), b),
    )
    c, d = (
        jnp.where(even, c, pltpu.roll(d, 32, 2)),
        jnp.where(even, pltpu.roll(c, 96, 2), d),
    )
    return a, b, c, d


def build_bands(row_taps, col_taps, a_hi, a_lo, at_hi, at_lo, b_both, bt_both, pad):
    pad[...] = jnp.zeros_like(pad)
    pad[0:8, 0:TAPS] = row_taps[...]
    pad[8:16, 0:TAPS] = col_taps[...]
    c = lax.broadcasted_iota(I32, (256, 256), 0)
    p = lax.broadcasted_iota(I32, (256, 256), 1)
    placed = (c & ~31) + ((c & 3) << 3) + ((c & 31) >> 2)
    permute = (p == placed).astype(F32).astype(BF16)

    def shifted(line):
        row = pad[pl.ds(line, 1), :]
        return pltpu.roll(jnp.broadcast_to(row, (128, 256)), 0, 1, stride=1, stride_axis=0)

    for k in range(KERNELS):
        rows = pl.ds(k * 128, 128)
        for part, a_out, at_out in zip(split(shifted(k)), (a_hi, a_lo), (at_hi, at_lo)):
            ordered = mm(part, permute)
            a_out[rows, :] = ordered.astype(BF16)
            at_out[:, rows] = ordered.T.astype(BF16)
        for i, part in enumerate(split(shifted(8 + k))):
            part = part.astype(F32)
            lanes = pl.ds(i * 128, 128)
            b_both[k, :, lanes] = part.T.astype(BF16)
            bt_both[k, 0:128, lanes] = part[:, 128:256].astype(BF16)
            bt_both[k, 128:256, lanes] = part[:, 0:128].astype(BF16)


def image_gradient(
    weight, wide, target, a_hi, a_lo, at_hi, at_lo, b_both, bt_both, out,
    x_hi, x_lo, y_hi, y_lo, fields, p_hi, p_lo, q_hi, q_lo,
):
    x_hi[192:256, :] = jnp.zeros((64, GROUPS * 128), BF16)
    x_lo[192:256, :] = jnp.zeros((64, GROUPS * 128), BF16)
    for g in range(GROUPS):
        turned = swap_blocks([wide[:, 4 * g + q] for q in range(4)])
        value = jnp.concatenate(turned, axis=1).reshape(192, 128)
        lanes = pl.ds(g * 128, 128)
        x_hi[0:192, lanes], x_lo[0:192, lanes] = split(value)
    for g in range(GROUPS):
        lanes = pl.ds(g * 128, 128)
        high, low = x_hi[:, lanes], x_lo[:, lanes]
        both = mm(a_hi[...], jnp.concatenate([high, low], axis=1))
        value = both[:, :128] + both[:, 128:] + mm(a_lo[...], high)
        y_hi[:, g], y_lo[:, g] = (v.reshape(KERNELS, 128, 128) for v in split(value))
    intensity = jnp.zeros((1024, 128), F32)
    for k in range(KERNELS):
        def window(ref):
            return jnp.concatenate(
                [ref[k, 0:8].reshape(1024, 128), ref[k, 1:9].reshape(1024, 128)], axis=1
            )
        both = mm(window(y_hi), b_both[k])
        field = both[:, :128] + both[:, 128:] + mm(window(y_lo), b_both[k, :, 0:128])
        fields[k] = field
        intensity = intensity + weight[k] * field * field
    wanted = jnp.concatenate([target[:, 128 * n:128 * n + 128] for n in range(8)], axis=0)
    resist = 1.0 / (1.0 + jnp.exp(-STEEPNESS * (intensity - THRESHOLD)))
    sensitivity = 2.0 * (resist - wanted) * STEEPNESS * resist * (1.0 - resist)
    for ref in (p_hi, p_lo):
        ref[0] = jnp.zeros((128, 128), BF16)
        ref[9] = jnp.zeros((128, 128), BF16)
    for k in range(KERNELS):
        product = (2.0 * weight[k]) * sensitivity * fields[k]
        p_hi[1:9], p_lo[1:9] = (v.reshape(8, 128, 128) for v in split(product))

        def window(ref):
            return jnp.concatenate(
                [ref[0:9].reshape(1152, 128), ref[1:10].reshape(1152, 128)], axis=1
            )
        both = mm(window(p_hi), bt_both[k])
        value = both[:, :128] + both[:, 128:] + mm(window(p_lo), bt_both[k, :, 0:128])
        high, low = split(value)
        for g in range(GROUPS):
            lanes = pl.ds(g * 128, 128)
            rows = pl.ds(k * 128, 128)
            q_hi[rows, lanes] = high[128 * g:128 * g + 128]
            q_lo[rows, lanes] = low[128 * g:128 * g + 128]
    for g in range(GROUPS):
        lanes = pl.ds(g * 128, 128)
        high, low = q_hi[:, lanes], q_lo[:, lanes]
        both = mm(at_hi[0:192, :], jnp.concatenate([high, low], axis=1))
        value = both[:, :128] + both[:, 128:] + mm(at_lo[0:192, :], high)
        value = value.reshape(6, 32, 128)
        turned = swap_blocks([value[:, 8 * s:8 * s + 8] for s in range(4)])
        for q in range(4):
            out[:, 4 * g + q] = turned[q]


def exists(at, counts, step):
    ok = None
    for a, count, d in zip(at, counts, step):
        if d:
            here = (a + d >= 0) if d < 0 else (a + d < count)
            ok = here if ok is None else jnp.logical_and(ok, here)
    return ok


def exchange(copy, at, counts):
    for i, (dr, dc) in enumerate(NEIGHBOURS):
        @pl.when(exists(at, counts, (dr, dc)))
        def _():
            copy(i, dr, dc).start()
    for i, (dr, dc) in enumerate(NEIGHBOURS):
        @pl.when(exists(at, counts, (dr, dc)))
        def _():
            copy(i, dr, dc).wait_send()

        @pl.when(exists(at, counts, (-dr, -dc)))
        def _():
            copy(i, dr, dc).wait_recv()


def hops(step):
    return sum(min(d, 4 - d) for d in step[:3])


STEPS = sorted((s for s in itertools.product(range(4), range(4), range(4), range(2)) if any(s)), key=lambda s: -hops(s))


def step_kernel(
    counts, weight, inst, cells, row_taps, col_taps, target, out,
    pad, mine, table, cells3, outgoing, arrived, index_v, index_s, where_v, where_s, tile_v, tile_s, wide,
    a_hi, a_lo, at_hi, at_lo, b_both, bt_both, taps_pad,
    x_hi, x_lo, y_hi, y_lo, fields, p_hi, p_lo, q_hi, q_lo,
    grad, halo_row, halo_col, halo_corner, own, back,
    table_send, table_recv, block_send, block_recv, cell_send, cell_recv, grad_send, grad_recv,
    halo_send, halo_recv, rim_send, rim_recv, local,
):
    row_count, col_count = counts
    total = row_count * col_count
    at = row, col = lax.axis_index("row"), lax.axis_index("col")
    me = row * col_count + col
    barrier = pltpu.get_barrier_semaphore()
    row_peers = [(row, lax.rem(col + i, col_count)) for i in range(1, col_count)]
    col_peers = [(lax.rem(row + i, row_count), col) for i in range(1, row_count)]

    def remote(source, target, send, recv, where):
        return pltpu.make_async_remote_copy(
            src_ref=source, dst_ref=target, send_sem=send, recv_sem=recv,
            device_id=where, device_id_type=MESH,
        )

    for a in (0, 5):
        wide[a] = jnp.zeros((WIDE, 8, 128), F32)
    for b in (0, 33, 34, 35):
        wide[1:5, b] = jnp.zeros((TILE_ROWS, 8, 128), F32)
    for ref in (halo_row, halo_col, halo_corner):
        ref[...] = jnp.zeros_like(ref)
    for where in row_peers + col_peers:
        pl.semaphore_signal(barrier, inc=1, device_id=where, device_id_type=MESH)
    pad[...] = jnp.zeros_like(pad)
    pad[0:TILE_ROWS, 0:TILE_COLS] = inst[...]
    lines = pad[...]
    line = lax.broadcasted_iota(I32, lines.shape, 0)
    flat = jnp.zeros((8, 128), I32)
    for a in range(TILE_ROWS):
        moved = pltpu.roll(lines, 32 * a, 1) if a else lines
        flat = flat + jnp.where(line == a, moved, 0)
    flat = jnp.sum(flat, axis=0, keepdims=True)
    mine[0] = flat
    table[me] = flat
    for r in range(8):
        cells3[:, r, :] = cells[:, 128 * r:128 * r + 128]
    pl.semaphore_wait(barrier, len(row_peers) + len(col_peers))

    for where in row_peers:
        remote(mine, table.at[pl.ds(me, 1)], table_send, table_recv, where).start()
    lane = lax.broadcasted_iota(I32, (128, 128), 1)
    sub = lax.broadcasted_iota(I32, (128, 128), 0)
    diagonal = lane == sub

    def as_row(column):
        return jnp.sum(jnp.where(diagonal, column, 0), axis=0, keepdims=True)
    owner = flat >> 5
    held = owner == sub
    first = jnp.min(jnp.where(held, lane, TILES), axis=1, keepdims=True)
    last = jnp.max(jnp.where(held, lane, -1), axis=1, keepdims=True)
    second = jnp.sum(jnp.where(held & (lane != first), 1, 0), axis=0, keepdims=True)
    tile_v[0:1, :] = as_row(jnp.minimum(first, TILES - 1))
    tile_v[1:2, :] = as_row(jnp.maximum(last, 0))
    where_v[...] = owner * 2 + second
    where_copy = pltpu.make_async_copy(where_v, where_s, local.at[0])
    tile_copy = pltpu.make_async_copy(tile_v, tile_s, local.at[1])
    where_copy.start()
    tile_copy.start()
    others = table.at[pl.ds(0, len(row_peers))]
    remote(others, others, table_send, table_recv, row_peers[0]).wait()
    block = table.at[pl.ds(row * col_count, col_count)]
    for where in col_peers:
        remote(block, block, block_send, block_recv, where).start()
    others = table.at[pl.ds(0, len(col_peers) * col_count)]
    remote(others, others, block_send, block_recv, col_peers[0]).wait()

    asked = table[...].reshape(128, 128)
    hit = (asked >> 5) == me
    key = lane * SLOTS + (asked & (SLOTS - 1))
    first = jnp.min(jnp.where(hit, key, TILES * SLOTS), axis=1, keepdims=True)
    last = jnp.max(jnp.where(hit, key, -1), axis=1, keepdims=True)
    chosen = (
        as_row(jnp.where(first < TILES * SLOTS, first & (SLOTS - 1), -1)),
        as_row(jnp.where(last > first, last & (SLOTS - 1), -1)),
    )
    for s in range(2):
        index_v[s:s + 1, :] = jnp.maximum(chosen[s], 0)
    cell = lax.broadcasted_iota(I32, (SLOTS, 128), 0)
    selector = jnp.concatenate([(cell == c).astype(F32).astype(BF16) for c in chosen], axis=1)
    index_copy = pltpu.make_async_copy(index_v, index_s, local.at[2])
    index_copy.start()

    core, z = lax.rem(row, 2), lax.rem(row // 2, 4)
    y, x = (row // 8) * 2 + lax.rem(col, 2), col // 2

    def everyone(source, index, landing, send, recv):
        for dx, dy, dz, dcore in STEPS:
            to_y = lax.rem(y + dy, 4)
            to_row = (to_y // 2) * 8 + lax.rem(z + dz, 4) * 2 + lax.rem(core + dcore, 2)
            to_col = lax.rem(x + dx, 4) * 2 + lax.rem(to_y, 2)
            peer = to_row * col_count + to_col
            for s in range(2):
                outgoing[2 * peer + s] = source[index[s, peer]]
            remote(
                outgoing.at[pl.ds(2 * peer, 2)], landing.at[pl.ds(2 * me, 2)], send, recv, (to_row, to_col)
            ).start()
        for s in range(2):
            landing[2 * me + s] = source[index[s, me]]

    def everyone_wait(landing, send, recv):
        others = pl.ds(0, 2 * (total - 1))
        remote(outgoing.at[others], landing.at[others], send, recv, row_peers[0]).wait()

    index_copy.wait()
    everyone(cells3, index_s, arrived, cell_send, cell_recv)
    where_copy.wait()
    tile_copy.wait()
    build_bands(row_taps, col_taps, a_hi, a_lo, at_hi, at_lo, b_both, bt_both, taps_pad)
    everyone_wait(arrived, cell_send, cell_recv)

    def put(t, carry):
        wide[1 + t // TILE_COLS, 1 + lax.rem(t, TILE_COLS)] = arrived[where_s[0, t]]
        return carry
    lax.fori_loop(0, TILES, put, 0, unroll=8)

    def halo(i, dr, dc):
        return remote(
            wide.at[span(dr, TILE_ROWS, True), span(dc, TILE_COLS, True)],
            wide.at[span(-dr, TILE_ROWS, False), span(-dc, TILE_COLS, False)],
            halo_send.at[i], halo_recv.at[i], (row + dr, col + dc),
        )
    exchange(halo, at, counts)

    image_gradient(
        weight, wide, target, a_hi, a_lo, at_hi, at_lo, b_both, bt_both, grad,
        x_hi, x_lo, y_hi, y_lo, fields, p_hi, p_lo, q_hi, q_lo,
    )

    def rim(i, dr, dc):
        side_row, side_col = 0 if dr < 0 else TILE_ROWS + 1, 0 if dc < 0 else TILE_COLS + 1
        if dr == 0:
            source, landing = grad.at[pl.ds(1, TILE_ROWS), side_col], halo_col.at[0 if dc < 0 else 1]
        elif dc == 0:
            source, landing = grad.at[side_row, pl.ds(1, TILE_COLS)], halo_row.at[0 if dr < 0 else 1]
        else:
            source, landing = grad.at[side_row, side_col], halo_corner.at[2 * (dr > 0) + (dc > 0)]
        return remote(source, landing, rim_send.at[i], rim_recv.at[i], (row + dr, col + dc))
    exchange(rim, at, counts)
    own[...] = grad[1:5, 1:33].reshape(TILES, 8, 128)
    own[96:128] = own[96:128] + halo_row[0]
    own[0:32] = own[0:32] + halo_row[1]
    for a in range(TILE_ROWS):
        t = TILE_COLS * a
        own[t + 31] = own[t + 31] + halo_col[0, a]
        own[t] = own[t] + halo_col[1, a]
    for i, t in enumerate((127, 96, 31, 0)):
        own[t] = own[t] + halo_corner[i]

    everyone(own, tile_s, back, grad_send, grad_recv)
    everyone_wait(back, grad_send, grad_recv)
    flat = back.reshape(2 * TILES * 8, 128)
    for r in range(8):
        value = jnp.concatenate(
            [flat[pl.ds(8 * s + r, 128, stride=16), :] for s in range(2)], axis=0
        )
        high, low = split(value)
        tail = (value - high.astype(F32) - low.astype(F32)).astype(BF16)
        parts = mm(selector, jnp.concatenate([high, low, tail], axis=1))
        total_r = parts[:, 0:128] + parts[:, 128:256] + parts[:, 256:384]
        lanes = slice(128 * r, 128 * r + 128)
        out[:, lanes] = cells[:, lanes] - STEP_RATE * total_r


def shards(counts, cells, instance_cell, target, row_taps, col_taps, kernel_weight):
    vmem = pltpu.VMEM
    smem = pltpu.SMEM
    dma = pltpu.SemaphoreType.DMA
    return pl.pallas_call(
        functools.partial(step_kernel, counts),
        name="gradient_step",
        out_shape=jax.ShapeDtypeStruct((SLOTS, 1024), F32),
        in_specs=[SCALARS] + [WHOLE] * 5,
        out_specs=WHOLE,
        scratch_shapes=[
            vmem((8, 128), I32), vmem((1, 1, 128), I32), vmem((128, 1, 128), I32),
            vmem((SLOTS, 8, 128), F32), vmem((256, 8, 128), F32), vmem((256, 8, 128), F32),
            vmem((2, 128), I32), smem((2, 128), I32), vmem((1, 128), I32), smem((1, 128), I32),
            vmem((2, 128), I32), smem((2, 128), I32), vmem((6, WIDE, 8, 128), F32),
            vmem((1024, 256), BF16), vmem((1024, 256), BF16), vmem((256, 1024), BF16), vmem((256, 1024), BF16),
            vmem((8, 256, 256), BF16), vmem((8, 256, 256), BF16), vmem((16, 256), F32),
            vmem((256, 1152), BF16), vmem((256, 1152), BF16),
            vmem((8, 9, 128, 128), BF16), vmem((8, 9, 128, 128), BF16),
            vmem((8, 1024, 128), F32),
            vmem((10, 128, 128), BF16), vmem((10, 128, 128), BF16),
            vmem((1024, 1152), BF16), vmem((1024, 1152), BF16),
            vmem((6, WIDE, 8, 128), F32),
            vmem((2, 32, 8, 128), F32), vmem((2, 4, 8, 128), F32), vmem((4, 8, 128), F32),
            vmem((TILES, 8, 128), F32), vmem((256, 8, 128), F32),
        ] + [dma] * 8 + [dma((8,))] * 4 + [dma((3,))],
        compiler_params=pltpu.CompilerParams(collective_id=0, has_side_effects=True),
    )(kernel_weight, instance_cell, cells, row_taps, col_taps, target)


def solution(mesh):
    placed = (P(("row", "col"), None), P("row", "col"), P("row", "col"), P(), P(), P())
    return jax.shard_map(
        functools.partial(shards, (mesh.shape["row"], mesh.shape["col"])),
        mesh=mesh, in_specs=placed, out_specs=P(("row", "col"), None), check_vma=False,
    )
```

```python
import functools
import itertools

import jax
import jax.numpy as jnp
from jax import lax
from jax.experimental import pallas as pl
from jax.experimental.pallas import tpu as pltpu
from jax.sharding import PartitionSpec as P

TILE = 32
TAPS = 65
KERNELS = 8
ROWS = 128
COLS = 1024
TILE_ROWS = 4
TILE_COLS = 32
TILES = 128
SLOTS = 32
WIDE = 36
GROUPS = 9
STEEPNESS = 4.0
THRESHOLD = 0.3
STEP_RATE = 0.5
MESH = pl.DeviceIdType.MESH
BF16 = jnp.bfloat16
F32 = jnp.float32
I32 = jnp.int32
WHOLE = pl.BlockSpec(memory_space=pltpu.VMEM)
SCALARS = pl.BlockSpec(memory_space=pltpu.SMEM)

NEIGHBOURS = tuple((dr, dc) for dr in (-1, 0, 1) for dc in (-1, 0, 1) if (dr, dc) != (0, 0))


def span(step, count, inside):
    if step == 0:
        return pl.ds(1, count)
    if step < 0:
        return pl.ds(1 if inside else 0, 1)
    return pl.ds(count if inside else count + 1, 1)


def split(value):
    high = value.astype(BF16)
    return high, (value - high.astype(F32)).astype(BF16)


def mm(a, b):
    return jnp.dot(a, b, preferred_element_type=F32)


def swap_blocks(vectors):
    lane = lax.broadcasted_iota(I32, vectors[0].shape, 2)
    low = lane < 64
    even = (lane & 32) == 0
    a, b, c, d = vectors
    a, c = (
        jnp.where(low, a, pltpu.roll(c, 64, 2)),
        jnp.where(low, pltpu.roll(a, 64, 2), c),
    )
    b, d = (
        jnp.where(low, b, pltpu.roll(d, 64, 2)),
        jnp.where(low, pltpu.roll(b, 64, 2), d),
    )
    a, b = (
        jnp.where(even, a, pltpu.roll(b, 32, 2)),
        jnp.where(even, pltpu.roll(a, 96, 2), b),
    )
    c, d = (
        jnp.where(even, c, pltpu.roll(d, 32, 2)),
        jnp.where(even, pltpu.roll(c, 96, 2), d),
    )
    return a, b, c, d


def build_bands(row_taps, col_taps, a_own, a_halo, at_own, at_halo, b_both, bt_both, pad):
    pad[...] = jnp.zeros_like(pad)
    pad[0:8, 0:TAPS] = row_taps[...]
    pad[8:16, 0:TAPS] = col_taps[...]
    c = lax.broadcasted_iota(I32, (256, 256), 0)
    p = lax.broadcasted_iota(I32, (256, 256), 1)
    inner = ((c & 3) << 3) + ((c & 31) >> 2)
    tile = c >> 5
    is_own = (tile >= 1) & (tile <= 4)
    own_at = jnp.where(is_own, 32 * tile - 32 + inner, -1024)
    halo_at = jnp.where(tile == 0, inner, jnp.where(tile == 5, 32 + inner, -1024))

    def ones(condition):
        return condition.astype(F32).astype(BF16)
    own_high, own_low = ones(p == own_at), ones(p == own_at + 128)
    halo_high, halo_low = ones((p == halo_at) | (p == halo_at + 128)), ones(p == halo_at + 64)

    def shifted(line):
        row = pad[pl.ds(line, 1), :]
        return pltpu.roll(jnp.broadcast_to(row, (128, 256)), 0, 1, stride=1, stride_axis=0)

    for k in range(KERNELS):
        rows = pl.ds(k * 128, 128)
        high, low = split(shifted(k))
        own = mm(high, own_high) + mm(low, own_low)
        halo = mm(high, halo_high) + mm(low, halo_low)
        a_own[rows, :] = own.astype(BF16)
        a_halo[rows, :] = halo.astype(BF16)
        at_own[:, rows] = own.T.astype(BF16)
        at_halo[:, rows] = halo.T[0:128].astype(BF16)
        for i, part in enumerate(split(shifted(8 + k))):
            part = part.astype(F32)
            lanes = pl.ds(i * 128, 128)
            b_both[k, :, lanes] = part.T.astype(BF16)
            bt_both[k, 0:128, lanes] = part[:, 128:256].astype(BF16)
            bt_both[k, 128:256, lanes] = part[:, 0:128].astype(BF16)


def lanes_of(g, count=1):
    return pl.ds(g * 128, 128 * count)


EARLY = (1, 3, 5)


def mask_own(g, wide, x_own, x_low):
    turned = swap_blocks([wide[1:5, 4 * g + q] for q in range(4)])
    high, low = split(jnp.concatenate(turned, axis=1).reshape(128, 128))
    x_own[0:128, lanes_of(g)] = high
    x_own[128:256, lanes_of(g)] = high
    x_low[:, lanes_of(g)] = low


def rows_own(wide, a_own, x_own, x_low, early):
    for i, g in enumerate(EARLY):
        for h in (g, g + 1):
            mask_own(h, wide, x_own, x_low)
        lanes = lanes_of(g, 2)
        early[i] = mm(a_own[...], x_own[:, lanes]) + mm(a_own[:, 0:128], x_low[:, lanes])
    mask_own(7, wide, x_own, x_low)


def forward(weight, wide, a_own, a_halo, b_both, x_own, x_low, x_halo, early, y_hi, y_lo, fields, power):
    for g in (0, 8):
        mask_own(g, wide, x_own, x_low)
    x_halo[192:256, :] = jnp.zeros((64, GROUPS * 128), BF16)
    for g in range(GROUPS):
        sides = [jnp.stack([wide[0, 4 * g + q], wide[5, 4 * g + q]]) for q in range(4)]
        value = jnp.concatenate(swap_blocks(sides), axis=1).reshape(64, 128)
        high, low = split(value)
        lanes = lanes_of(g)
        x_halo[0:64, lanes] = high
        x_halo[64:128, lanes] = high
        x_halo[128:192, lanes] = low

    def keep(g, value):
        y_hi[:, g], y_lo[:, g] = (v.reshape(KERNELS, 128, 128) for v in split(value))
    lanes = lanes_of(7, 2)
    value = (
        mm(a_own[...], x_own[:, lanes]) + mm(a_own[:, 0:128], x_low[:, lanes]) + mm(a_halo[...], x_halo[:, lanes])
    )
    for h in range(2):
        keep(7 + h, value[:, 128 * h:128 * h + 128])
    lanes = lanes_of(0)
    beside = jnp.concatenate([x_low[:, lanes], jnp.zeros((128, 128), BF16)], axis=0)
    both = mm(a_own[...], jnp.concatenate([x_own[:, lanes], beside], axis=1))
    keep(0, both[:, 0:128] + both[:, 128:256] + mm(a_halo[...], x_halo[:, lanes]))
    for i, g in enumerate(EARLY):
        value = early[i] + mm(a_halo[...], x_halo[:, lanes_of(g, 2)])
        for h in range(2):
            keep(g + h, value[:, 128 * h:128 * h + 128])
    for k in range(KERNELS):
        def window(ref):
            return jnp.concatenate(
                [ref[k, 0:8].reshape(1024, 128), ref[k, 1:9].reshape(1024, 128)], axis=1
            )
        both = mm(window(y_hi), b_both[k])
        field = both[:, :128] + both[:, 128:] + mm(window(y_lo), b_both[k, :, 0:128])
        fields[k] = field
        share = weight[k] * field * field
        power[...] = share if k == 0 else power[...] + share


def adjoint_columns(weight, target, bt_both, fields, power, p_hi, p_lo, q_hi, q_lo):
    for n in range(8):
        part = pl.ds(128 * n, 128)
        wanted = target[:, part]
        resist = 1.0 / (1.0 + jnp.exp(-STEEPNESS * (power[part, :] - THRESHOLD)))
        power[part, :] = (2.0 * STEEPNESS * 2.0) * (resist - wanted) * resist * (1.0 - resist)
    for k in range(KERNELS):
        high, low = p_hi.at[k % 2], p_lo.at[k % 2]
        product = weight[k] * power[...] * fields[k]
        high[1:9], low[1:9] = (v.reshape(8, 128, 128) for v in split(product))

        def window(ref):
            return jnp.concatenate(
                [ref[0:9].reshape(1152, 128), ref[1:10].reshape(1152, 128)], axis=1
            )
        both = mm(window(high), bt_both[k])
        value = both[:, :128] + both[:, 128:] + mm(window(low), bt_both[k, :, 0:128])
        high, low = split(value)
        for g in range(GROUPS):
            rows = pl.ds(k * 128, 128)
            q_hi[rows, lanes_of(g)] = high[128 * g:128 * g + 128]
            q_lo[rows, lanes_of(g)] = low[128 * g:128 * g + 128]


def adjoint_rows(bands, count, g, q_hi, q_lo):
    tiles = []
    if g == GROUPS - 1:
        lanes = lanes_of(g)
        both = mm(bands[...], jnp.concatenate([q_hi[:, lanes], q_lo[:, lanes]], axis=1))
        both = both[:, 0:128] + both[:, 128:256]
        parts = [both[0:count] + both[count:2 * count]]
    else:
        lanes = lanes_of(g, 2)
        both = mm(bands[...], q_hi[:, lanes])
        value = both[0:count] + both[count:2 * count] + mm(bands[0:count, :], q_lo[:, lanes])
        parts = [value[:, 0:128], value[:, 128:256]]
    for h, value in enumerate(parts):
        value = value.reshape(count // 32, 32, 128)
        turned = swap_blocks([value[:, 8 * s:8 * s + 8] for s in range(4)])
        tiles += [(4 * (g + h) + q, turned[q]) for q in range(4)]
    return tiles


def exists(at, counts, step):
    ok = None
    for a, count, d in zip(at, counts, step):
        if d:
            here = (a + d >= 0) if d < 0 else (a + d < count)
            ok = here if ok is None else jnp.logical_and(ok, here)
    return ok


def start_copies(copy, at, counts, which):
    for i in which:
        @pl.when(exists(at, counts, NEIGHBOURS[i]))
        def _():
            copy(i, *NEIGHBOURS[i]).start()


def wait_copies(copy, at, counts):
    for i, (dr, dc) in enumerate(NEIGHBOURS):
        @pl.when(exists(at, counts, (dr, dc)))
        def _():
            copy(i, dr, dc).wait_send()

        @pl.when(exists(at, counts, (-dr, -dc)))
        def _():
            copy(i, dr, dc).wait_recv()


ACROSS = sorted((i for i, (dr, dc) in enumerate(NEIGHBOURS) if dr), key=lambda i: NEIGHBOURS[i][1] == 0)
ALONG = [i for i, (dr, dc) in enumerate(NEIGHBOURS) if not dr]


def hops(step):
    return sum(min(d, 4 - d) for d in step[:3])


STEPS = sorted((s for s in itertools.product(range(4), range(4), range(4), range(2)) if any(s)), key=lambda s: -hops(s))


def step_kernel(
    counts, weight, inst, cells, row_taps, col_taps, target_hbm, out,
    pad, table, cells3, outgoing, arrived, index_v, index_s, where_v, where_s, tile_v, tile_s, wide, target,
    a_own, a_halo, at_own, at_halo, b_both, bt_both, taps_pad,
    x_own, x_low, x_halo, early, y_hi, y_lo, fields, power, p_hi, p_lo, q_hi, q_lo,
    rim_row, rim_col, halo_row, halo_col, halo_corner, own, back,
    table_send, table_recv, block_send, block_recv, cell_send, cell_recv, grad_send, grad_recv,
    halo_send, halo_recv, rim_send, rim_recv, local,
):
    row_count, col_count = counts
    total = row_count * col_count
    at = row, col = lax.axis_index("row"), lax.axis_index("col")
    me = row * col_count + col
    barrier = pltpu.get_barrier_semaphore()
    core, z = lax.rem(row, 2), lax.rem(row // 2, 4)
    y, x = (row // 8) * 2 + lax.rem(col, 2), col // 2

    def device(step):
        dx, dy, dz, dcore = step
        to = lax.rem(x + dx, 4), lax.rem(y + dy, 4), lax.rem(z + dz, 4), lax.rem(core + dcore, 2)
        where = (to[1] // 2) * 8 + to[2] * 2 + to[3], to[0] * 2 + lax.rem(to[1], 2)
        return where, ((to[0] * 4 + to[1]) * 4 + to[2]) * 2 + to[3]
    rank = ((x * 4 + y) * 4 + z) * 2 + core
    near = [device(s)[0] for s in STEPS if s[0] == s[1] == 0]
    far = [device(s)[0] for s in STEPS if s[2] == s[3] == 0]

    def remote(source, landing, send, recv, where):
        return pltpu.make_async_remote_copy(
            src_ref=source, dst_ref=landing, send_sem=send, recv_sem=recv,
            device_id=where, device_id_type=MESH,
        )

    for a in (0, 5):
        wide[a] = jnp.zeros((WIDE, 8, 128), F32)
    for b in (0, 33, 34, 35):
        wide[1:5, b] = jnp.zeros((TILE_ROWS, 8, 128), F32)
    for ref in (halo_row, halo_col, halo_corner):
        ref[...] = jnp.zeros_like(ref)
    for where in far + near:
        pl.semaphore_signal(barrier, inc=1, device_id=where, device_id_type=MESH)
    target_copy = pltpu.make_async_copy(target_hbm, target, local.at[3])
    target_copy.start()
    pad[...] = jnp.zeros_like(pad)
    pad[0:TILE_ROWS, 0:TILE_COLS] = inst[...]
    lines = pad[...]
    line = lax.broadcasted_iota(I32, lines.shape, 0)
    flat = jnp.zeros((8, 128), I32)
    for a in range(TILE_ROWS):
        moved = pltpu.roll(lines, 32 * a, 1) if a else lines
        flat = flat + jnp.where(line == a, moved, 0)
    flat = jnp.sum(flat, axis=0, keepdims=True)
    table[rank] = flat
    for r in range(8):
        cells3[:, r, :] = cells[:, 128 * r:128 * r + 128]
    lane = lax.broadcasted_iota(I32, (128, 128), 1)
    sub = lax.broadcasted_iota(I32, (128, 128), 0)
    diagonal = lane == sub

    def as_row(column):
        return jnp.sum(jnp.where(diagonal, column, 0), axis=0, keepdims=True)
    owner = flat >> 5
    held = owner == sub
    first = jnp.min(jnp.where(held, lane, TILES), axis=1, keepdims=True)
    last = jnp.max(jnp.where(held, lane, -1), axis=1, keepdims=True)
    second = jnp.sum(jnp.where(held & (lane != first), 1, 0), axis=0, keepdims=True)
    tile_v[0:1, :] = as_row(jnp.minimum(first, TILES - 1))
    tile_v[1:2, :] = as_row(jnp.maximum(last, 0))
    where_v[...] = owner * 2 + second
    where_copy = pltpu.make_async_copy(where_v, where_s, local.at[0])
    tile_copy = pltpu.make_async_copy(tile_v, tile_s, local.at[1])
    where_copy.start()
    tile_copy.start()
    pl.semaphore_wait(barrier, len(near) + len(far))

    mine = table.at[pl.ds(rank, 1)]
    for where in near:
        remote(mine, mine, table_send, table_recv, where).start()
    others = table.at[pl.ds(0, len(near))]
    remote(others, others, table_send, table_recv, near[0]).wait()
    block = table.at[pl.ds((x * 4 + y) * 8, 8)]
    for where in far:
        remote(block, block, block_send, block_recv, where).start()
    others = table.at[pl.ds(0, len(far) * 8)]
    remote(others, others, block_send, block_recv, far[0]).wait()

    asked = table[...].reshape(128, 128)
    hit = (asked >> 5) == me
    key = lane * SLOTS + (asked & (SLOTS - 1))
    first = jnp.min(jnp.where(hit, key, TILES * SLOTS), axis=1, keepdims=True)
    last = jnp.max(jnp.where(hit, key, -1), axis=1, keepdims=True)
    chosen = (
        as_row(jnp.where(first < TILES * SLOTS, first & (SLOTS - 1), -1)),
        as_row(jnp.where(last > first, last & (SLOTS - 1), -1)),
    )
    for s in range(2):
        index_v[s:s + 1, :] = jnp.maximum(chosen[s], 0)
    cell = lax.broadcasted_iota(I32, (SLOTS, 128), 0)
    selector = jnp.concatenate([(cell == c).astype(F32).astype(BF16) for c in chosen], axis=1)
    index_copy = pltpu.make_async_copy(index_v, index_s, local.at[2])
    index_copy.start()

    def everyone(source, index, by_rank, landing, place, send, recv):
        for i, step in enumerate(STEPS):
            where, to_rank = device(step)
            peer = to_rank if by_rank else where[0] * col_count + where[1]
            for s in range(2):
                outgoing[2 * i + s] = source[index[s, peer]]
            remote(
                outgoing.at[pl.ds(2 * i, 2)], landing.at[pl.ds(2 * place, 2)], send, recv, where
            ).start()
        for s in range(2):
            landing[2 * place + s] = source[index[s, rank if by_rank else me]]

    def everyone_wait(landing, send, recv):
        others = pl.ds(0, 2 * (total - 1))
        remote(outgoing.at[others], landing.at[others], send, recv, near[0]).wait()

    index_copy.wait()
    everyone(cells3, index_s, True, arrived, me, cell_send, cell_recv)
    where_copy.wait()
    tile_copy.wait()
    target_copy.wait()
    build_bands(row_taps, col_taps, a_own, a_halo, at_own, at_halo, b_both, bt_both, taps_pad)
    for ref in (p_hi, p_lo):
        for parity in range(2):
            ref[parity, 0] = jnp.zeros((128, 128), BF16)
            ref[parity, 9] = jnp.zeros((128, 128), BF16)
    everyone_wait(arrived, cell_send, cell_recv)

    def put(t, carry):
        wide[1 + t // TILE_COLS, 1 + lax.rem(t, TILE_COLS)] = arrived[where_s[0, t]]
        return carry
    lax.fori_loop(0, TILES, put, 0, unroll=8)

    def halo(i, dr, dc):
        return remote(
            wide.at[span(dr, TILE_ROWS, True), span(dc, TILE_COLS, True)],
            wide.at[span(-dr, TILE_ROWS, False), span(-dc, TILE_COLS, False)],
            halo_send.at[i], halo_recv.at[i], (row + dr, col + dc),
        )
    start_copies(halo, at, counts, ACROSS + ALONG)
    rows_own(wide, a_own, x_own, x_low, early)
    wait_copies(halo, at, counts)

    forward(weight, wide, a_own, a_halo, b_both, x_own, x_low, x_halo, early, y_hi, y_lo, fields, power)
    adjoint_columns(weight, target, bt_both, fields, power, p_hi, p_lo, q_hi, q_lo)

    def rim(i, dr, dc):
        side_row, side_col = int(dr > 0), 0 if dc < 0 else TILE_COLS + 1
        if dr == 0:
            source, landing = rim_col.at[int(dc > 0)], halo_col.at[int(dc > 0)]
        elif dc == 0:
            source, landing = rim_row.at[side_row, pl.ds(1, TILE_COLS)], halo_row.at[side_row]
        else:
            source, landing = rim_row.at[side_row, side_col], halo_corner.at[2 * side_row + int(dc > 0)]
        return remote(source, landing, rim_send.at[i], rim_recv.at[i], (row + dr, col + dc))

    for g in (0, 2, 4, 6, 8):
        for c, tiles in adjoint_rows(at_halo, 64, g, q_hi, q_lo):
            rim_row[:, c] = tiles
    start_copies(rim, at, counts, ACROSS)
    for g in (0, 8, 2, 4, 6):
        for c, tiles in adjoint_rows(at_own, 128, g, q_hi, q_lo):
            if c in (0, TILE_COLS + 1):
                rim_col[int(c > 0)] = tiles
            elif c <= TILE_COLS:
                for a in range(TILE_ROWS):
                    own[TILE_COLS * a + c - 1] = tiles[a]
        if g == 8:
            start_copies(rim, at, counts, ALONG)
    wait_copies(rim, at, counts)
    own[96:128] = own[96:128] + halo_row[0]
    own[0:32] = own[0:32] + halo_row[1]
    for a in range(TILE_ROWS):
        t = TILE_COLS * a
        own[t + 31] = own[t + 31] + halo_col[0, a]
        own[t] = own[t] + halo_col[1, a]
    for i, t in enumerate((127, 96, 31, 0)):
        own[t] = own[t] + halo_corner[i]

    everyone(own, tile_s, False, back, rank, grad_send, grad_recv)
    everyone_wait(back, grad_send, grad_recv)
    flat = back.reshape(2 * TILES * 8, 128)
    for r in range(8):
        value = jnp.concatenate(
            [flat[pl.ds(8 * s + r, 128, stride=16), :] for s in range(2)], axis=0
        )
        high, low = split(value)
        tail = (value - high.astype(F32) - low.astype(F32)).astype(BF16)
        parts = mm(selector, jnp.concatenate([high, low, tail], axis=1))
        total_r = parts[:, 0:128] + parts[:, 128:256] + parts[:, 256:384]
        lanes = slice(128 * r, 128 * r + 128)
        out[:, lanes] = cells[:, lanes] - STEP_RATE * total_r


def shards(counts, cells, instance_cell, target, row_taps, col_taps, kernel_weight):
    vmem = pltpu.VMEM
    smem = pltpu.SMEM
    dma = pltpu.SemaphoreType.DMA
    return pl.pallas_call(
        functools.partial(step_kernel, counts),
        name="gradient_step",
        out_shape=jax.ShapeDtypeStruct((SLOTS, 1024), F32),
        in_specs=[SCALARS] + [WHOLE] * 4 + [pl.BlockSpec(memory_space=pl.ANY)],
        out_specs=WHOLE,
        scratch_shapes=[
            vmem((8, 128), I32), vmem((128, 1, 128), I32),
            vmem((SLOTS, 8, 128), F32), vmem((256, 8, 128), F32), vmem((256, 8, 128), F32),
            vmem((2, 128), I32), smem((2, 128), I32), vmem((1, 128), I32), smem((1, 128), I32),
            vmem((2, 128), I32), smem((2, 128), I32), vmem((6, WIDE, 8, 128), F32), vmem((ROWS, COLS), F32),
            vmem((1024, 256), BF16), vmem((1024, 256), BF16), vmem((256, 1024), BF16), vmem((128, 1024), BF16),
            vmem((8, 256, 256), BF16), vmem((8, 256, 256), BF16), vmem((16, 256), F32),
            vmem((256, 1152), BF16), vmem((128, 1152), BF16), vmem((256, 1152), BF16),
            vmem((3, 1024, 256), F32),
            vmem((8, 9, 128, 128), BF16), vmem((8, 9, 128, 128), BF16),
            vmem((8, 1024, 128), F32), vmem((1024, 128), F32),
            vmem((2, 10, 128, 128), BF16), vmem((2, 10, 128, 128), BF16),
            vmem((1024, 1152), BF16), vmem((1024, 1152), BF16),
            vmem((2, WIDE, 8, 128), F32), vmem((2, 4, 8, 128), F32),
            vmem((2, 32, 8, 128), F32), vmem((2, 4, 8, 128), F32), vmem((4, 8, 128), F32),
            vmem((TILES, 8, 128), F32), vmem((256, 8, 128), F32),
        ] + [dma] * 8 + [dma((8,))] * 4 + [dma((4,))],
        compiler_params=pltpu.CompilerParams(collective_id=0, has_side_effects=True),
    )(kernel_weight, instance_cell, cells, row_taps, col_taps, target)


def solution(mesh):
    placed = (P(("row", "col"), None), P("row", "col"), P("row", "col"), P(), P(), P())
    return jax.shard_map(
        functools.partial(shards, (mesh.shape["row"], mesh.shape["col"])),
        mesh=mesh, in_specs=placed, out_specs=P(("row", "col"), None), check_vma=False,
    )
```

```python
import functools
import itertools

import jax
import jax.numpy as jnp
from jax import lax
from jax.experimental import pallas as pl
from jax.experimental.pallas import tpu as pltpu
from jax.sharding import PartitionSpec as P

TILE = 32
TAPS = 65
KERNELS = 8
ROWS = 128
COLS = 1024
TILE_ROWS = 4
TILE_COLS = 32
TILES = 128
SLOTS = 32
WIDE = 36
GROUPS = 9
STEEPNESS = 4.0
THRESHOLD = 0.3
STEP_RATE = 0.5
MESH = pl.DeviceIdType.MESH
BF16 = jnp.bfloat16
F32 = jnp.float32
I32 = jnp.int32
WHOLE = pl.BlockSpec(memory_space=pltpu.VMEM)
SCALARS = pl.BlockSpec(memory_space=pltpu.SMEM)

NEIGHBOURS = tuple((dr, dc) for dr in (-1, 0, 1) for dc in (-1, 0, 1) if (dr, dc) != (0, 0))


def span(step, count, inside):
    if step == 0:
        return pl.ds(1, count)
    if step < 0:
        return pl.ds(1 if inside else 0, 1)
    return pl.ds(count if inside else count + 1, 1)


def split(value):
    high = value.astype(BF16)
    return high, (value - high.astype(F32)).astype(BF16)


def mm(a, b):
    return jnp.dot(a, b, preferred_element_type=F32)


def swap_blocks(vectors):
    lane = lax.broadcasted_iota(I32, vectors[0].shape, 2)
    low = lane < 64
    even = (lane & 32) == 0
    a, b, c, d = vectors
    a, c = (
        jnp.where(low, a, pltpu.roll(c, 64, 2)),
        jnp.where(low, pltpu.roll(a, 64, 2), c),
    )
    b, d = (
        jnp.where(low, b, pltpu.roll(d, 64, 2)),
        jnp.where(low, pltpu.roll(b, 64, 2), d),
    )
    a, b = (
        jnp.where(even, a, pltpu.roll(b, 32, 2)),
        jnp.where(even, pltpu.roll(a, 96, 2), b),
    )
    c, d = (
        jnp.where(even, c, pltpu.roll(d, 32, 2)),
        jnp.where(even, pltpu.roll(c, 96, 2), d),
    )
    return a, b, c, d


def build_bands(row_taps, col_taps, a_own, a_halo, at_own, at_rim, b_both, bt_both, pad):
    pad[...] = jnp.zeros_like(pad)
    pad[0:8, 0:TAPS] = row_taps[...]
    pad[8:16, 0:TAPS] = col_taps[...]
    c = lax.broadcasted_iota(I32, (256, 256), 0)
    p = lax.broadcasted_iota(I32, (256, 256), 1)
    inner = ((c & 3) << 3) + ((c & 31) >> 2)
    tile = c >> 5
    is_own = (tile >= 1) & (tile <= 4)
    own_at = jnp.where(is_own, 32 * tile - 32 + inner, -1024)
    halo_at = jnp.where(tile == 0, inner, jnp.where(tile == 5, 32 + inner, -1024))

    def ones(condition):
        return condition.astype(F32).astype(BF16)
    own_high, own_low = ones(p == own_at), ones(p == own_at + 128)
    halo_high, halo_low = ones((p == halo_at) | (p == halo_at + 128)), ones(p == halo_at + 64)

    def shifted(line):
        row = pad[pl.ds(line, 1), :]
        return pltpu.roll(jnp.broadcast_to(row, (128, 256)), 0, 1, stride=1, stride_axis=0)

    for k in range(KERNELS):
        rows = pl.ds(k * 128, 128)
        high, low = split(shifted(k))
        own = mm(high, own_high) + mm(low, own_low)
        halo = mm(high, halo_high) + mm(low, halo_low)
        a_own[rows, :] = own.astype(BF16)
        a_halo[rows, :] = halo.astype(BF16)
        at_own[:, rows] = own.T.astype(BF16)
        turned = halo.T
        for h in range(2):
            at_rim[k, :, 128 * h:128 * h + 128] = turned[0:128].astype(BF16)
        for i, part in enumerate(split(shifted(8 + k))):
            part = part.astype(F32)
            lanes = pl.ds(i * 128, 128)
            b_both[k, :, lanes] = part.T.astype(BF16)
            bt_both[k, 0:128, lanes] = part[:, 128:256].astype(BF16)
            bt_both[k, 128:256, lanes] = part[:, 0:128].astype(BF16)


def lanes_of(g, count=1):
    return pl.ds(g * 128, 128 * count)


EARLY = (1, 3, 5)


def mask_own(g, wide, x_own, x_low):
    turned = swap_blocks([wide[1:5, 4 * g + q] for q in range(4)])
    high, low = split(jnp.concatenate(turned, axis=1).reshape(128, 128))
    x_own[0:128, lanes_of(g)] = high
    x_own[128:256, lanes_of(g)] = high
    x_low[:, lanes_of(g)] = low


def rows_own(wide, a_own, x_own, x_low, early):
    for i, g in enumerate(EARLY):
        for h in (g, g + 1):
            mask_own(h, wide, x_own, x_low)
        lanes = lanes_of(g, 2)
        early[i] = mm(a_own[...], x_own[:, lanes]) + mm(a_own[:, 0:128], x_low[:, lanes])
    mask_own(7, wide, x_own, x_low)


def forward(weight, wide, a_own, a_halo, b_both, x_own, x_low, x_halo, early, y_hi, y_lo, fields, power):
    for g in (0, 8):
        mask_own(g, wide, x_own, x_low)
    x_halo[192:256, :] = jnp.zeros((64, GROUPS * 128), BF16)
    for g in range(GROUPS):
        sides = [jnp.stack([wide[0, 4 * g + q], wide[5, 4 * g + q]]) for q in range(4)]
        value = jnp.concatenate(swap_blocks(sides), axis=1).reshape(64, 128)
        high, low = split(value)
        lanes = lanes_of(g)
        x_halo[0:64, lanes] = high
        x_halo[64:128, lanes] = high
        x_halo[128:192, lanes] = low

    def keep(g, value):
        y_hi[:, g], y_lo[:, g] = (v.reshape(KERNELS, 128, 128) for v in split(value))
    lanes = lanes_of(7, 2)
    value = (
        mm(a_own[...], x_own[:, lanes]) + mm(a_own[:, 0:128], x_low[:, lanes]) + mm(a_halo[...], x_halo[:, lanes])
    )
    for h in range(2):
        keep(7 + h, value[:, 128 * h:128 * h + 128])
    lanes = lanes_of(0)
    beside = jnp.concatenate([x_low[:, lanes], jnp.zeros((128, 128), BF16)], axis=0)
    both = mm(a_own[...], jnp.concatenate([x_own[:, lanes], beside], axis=1))
    keep(0, both[:, 0:128] + both[:, 128:256] + mm(a_halo[...], x_halo[:, lanes]))
    for i, g in enumerate(EARLY):
        value = early[i] + mm(a_halo[...], x_halo[:, lanes_of(g, 2)])
        for h in range(2):
            keep(g + h, value[:, 128 * h:128 * h + 128])
    for k in range(KERNELS):
        def window(ref):
            return jnp.concatenate(
                [ref[k, 0:8].reshape(1024, 128), ref[k, 1:9].reshape(1024, 128)], axis=1
            )
        both = mm(window(y_hi), b_both[k])
        field = both[:, :128] + both[:, 128:] + mm(window(y_lo), b_both[k, :, 0:128])
        fields[k] = field
        share = weight[k] * field * field
        power[...] = share if k == 0 else power[...] + share


def products(weight, target, fields, power, p_hi, p_lo):
    for n in range(8):
        part = pl.ds(128 * n, 128)
        wanted = target[:, part]
        resist = 1.0 / (1.0 + jnp.exp(-STEEPNESS * (power[part, :] - THRESHOLD)))
        power[part, :] = (2.0 * STEEPNESS * 2.0) * (resist - wanted) * resist * (1.0 - resist)
    for k in range(KERNELS):
        product = weight[k] * power[...] * fields[k]
        p_hi[k, 1:9], p_lo[k, 1:9] = (v.reshape(8, 128, 128) for v in split(product))


def windows(ref, start, count):
    rows = count * ref.shape[1]
    return jnp.concatenate(
        [ref[start:start + count].reshape(rows, 128), ref[start + 1:start + 1 + count].reshape(rows, 128)], axis=1
    )


def adjoint_rim(at_rim, bt_both, p_hi, p_lo, z_hi, z_lo):
    total = jnp.zeros((64 * GROUPS, 128), F32)
    for k in range(KERNELS):
        high, low = z_hi.at[k % 2], z_lo.at[k % 2]
        for n in (1, 3, 5, 7):
            upper = jnp.concatenate([p_hi[k, n], p_hi[k, n + 1]], axis=1)
            lower = jnp.concatenate([p_lo[k, n], p_lo[k, n + 1]], axis=1)
            both = mm(at_rim[k], jnp.concatenate([upper, lower], axis=0))
            value = both[0:64] + both[64:128]
            for h in range(2):
                high[n + h], low[n + h] = split(value[:, 128 * h:128 * h + 128])
        both = mm(windows(high, 0, GROUPS), bt_both[k])
        total = total + both[:, :128] + both[:, 128:] + mm(windows(low, 0, GROUPS), bt_both[k, :, 0:128])
    tiles = []
    for g in range(GROUPS):
        tiles += as_tiles(total[64 * g:64 * g + 64], g)
    return tiles


def as_tiles(value, g):
    value = value.reshape(value.shape[0] // 32, 32, 128)
    turned = swap_blocks([value[:, 8 * s:8 * s + 8] for s in range(4)])
    return [(4 * g + q, turned[q]) for q in range(4)]


def adjoint_columns(bt_both, p_hi, p_lo, q_hi, q_lo, groups):
    for k in range(KERNELS):
        def window(ref):
            return jnp.concatenate([windows(ref.at[k], start, count) for start, count in groups], axis=0)
        both = mm(window(p_hi), bt_both[k])
        value = both[:, :128] + both[:, 128:] + mm(window(p_lo), bt_both[k, :, 0:128])
        high, low = split(value)
        rows = pl.ds(k * 128, 128)
        for i, g in enumerate(g for start, count in groups for g in range(start, start + count)):
            q_hi[rows, lanes_of(g)] = high[128 * i:128 * i + 128]
            q_lo[rows, lanes_of(g)] = low[128 * i:128 * i + 128]


def adjoint_rows(bands, g, count, q_hi, q_lo):
    lanes = lanes_of(g, count)
    if count == 1:
        both = mm(bands[...], jnp.concatenate([q_hi[:, lanes], q_lo[:, lanes]], axis=1))
        both = both[:, 0:128] + both[:, 128:256]
        return as_tiles(both[0:128] + both[128:256], g)
    both = mm(bands[...], q_hi[:, lanes])
    value = both[0:128] + both[128:256] + mm(bands[0:128, :], q_lo[:, lanes])
    return as_tiles(value[:, 0:128], g) + as_tiles(value[:, 128:256], g + 1)


def exists(at, counts, step):
    ok = None
    for a, count, d in zip(at, counts, step):
        if d:
            here = (a + d >= 0) if d < 0 else (a + d < count)
            ok = here if ok is None else jnp.logical_and(ok, here)
    return ok


def start_copies(copy, at, counts, which):
    for i in which:
        @pl.when(exists(at, counts, NEIGHBOURS[i]))
        def _():
            copy(i, *NEIGHBOURS[i]).start()


def wait_copies(copy, at, counts):
    for i, (dr, dc) in enumerate(NEIGHBOURS):
        @pl.when(exists(at, counts, (dr, dc)))
        def _():
            copy(i, dr, dc).wait_send()

        @pl.when(exists(at, counts, (-dr, -dc)))
        def _():
            copy(i, dr, dc).wait_recv()


ACROSS = sorted((i for i, (dr, dc) in enumerate(NEIGHBOURS) if dr), key=lambda i: NEIGHBOURS[i][1] == 0)
ALONG = [i for i, (dr, dc) in enumerate(NEIGHBOURS) if not dr]


def hops(step):
    return sum(min(d, 4 - d) for d in step[:3])


STEPS = sorted((s for s in itertools.product(range(4), range(4), range(4), range(2)) if any(s)), key=lambda s: -hops(s))


def step_kernel(
    counts, weight, inst, cells, row_taps, col_taps, target_hbm, out,
    pad, table, cells3, outgoing, arrived, index_v, index_s, where_v, where_s, tile_v, tile_s, wide, target,
    a_own, a_halo, at_own, at_rim, b_both, bt_both, taps_pad,
    x_own, x_low, x_halo, early, y_hi, y_lo, fields, power, p_hi, p_lo, z_hi, z_lo, q_hi, q_lo,
    rim_row, rim_col, halo_row, halo_col, halo_corner, own, back,
    table_send, table_recv, block_send, block_recv, cell_send, cell_recv, grad_send, grad_recv,
    halo_send, halo_recv, rim_send, rim_recv, local,
):
    row_count, col_count = counts
    total = row_count * col_count
    at = row, col = lax.axis_index("row"), lax.axis_index("col")
    me = row * col_count + col
    barrier = pltpu.get_barrier_semaphore()
    core, z = lax.rem(row, 2), lax.rem(row // 2, 4)
    y, x = (row // 8) * 2 + lax.rem(col, 2), col // 2

    def device(step):
        dx, dy, dz, dcore = step
        to = lax.rem(x + dx, 4), lax.rem(y + dy, 4), lax.rem(z + dz, 4), lax.rem(core + dcore, 2)
        where = (to[1] // 2) * 8 + to[2] * 2 + to[3], to[0] * 2 + lax.rem(to[1], 2)
        return where, ((to[0] * 4 + to[1]) * 4 + to[2]) * 2 + to[3]
    rank = ((x * 4 + y) * 4 + z) * 2 + core
    near = [device(s)[0] for s in STEPS if s[0] == s[1] == 0]
    far = [device(s)[0] for s in STEPS if s[2] == s[3] == 0]

    def remote(source, landing, send, recv, where):
        return pltpu.make_async_remote_copy(
            src_ref=source, dst_ref=landing, send_sem=send, recv_sem=recv,
            device_id=where, device_id_type=MESH,
        )

    for a in (0, 5):
        wide[a] = jnp.zeros((WIDE, 8, 128), F32)
    for b in (0, 33, 34, 35):
        wide[1:5, b] = jnp.zeros((TILE_ROWS, 8, 128), F32)
    for ref in (halo_row, halo_col, halo_corner):
        ref[...] = jnp.zeros_like(ref)
    for where in far + near:
        pl.semaphore_signal(barrier, inc=1, device_id=where, device_id_type=MESH)
    target_copy = pltpu.make_async_copy(target_hbm, target, local.at[3])
    target_copy.start()
    pad[...] = jnp.zeros_like(pad)
    pad[0:TILE_ROWS, 0:TILE_COLS] = inst[...]
    lines = pad[...]
    line = lax.broadcasted_iota(I32, lines.shape, 0)
    flat = jnp.zeros((8, 128), I32)
    for a in range(TILE_ROWS):
        moved = pltpu.roll(lines, 32 * a, 1) if a else lines
        flat = flat + jnp.where(line == a, moved, 0)
    flat = jnp.sum(flat, axis=0, keepdims=True)
    table[rank] = flat
    for r in range(8):
        cells3[:, r, :] = cells[:, 128 * r:128 * r + 128]
    lane = lax.broadcasted_iota(I32, (128, 128), 1)
    sub = lax.broadcasted_iota(I32, (128, 128), 0)
    diagonal = lane == sub

    def as_row(column):
        return jnp.sum(jnp.where(diagonal, column, 0), axis=0, keepdims=True)
    owner = flat >> 5
    held = owner == sub
    first = jnp.min(jnp.where(held, lane, TILES), axis=1, keepdims=True)
    last = jnp.max(jnp.where(held, lane, -1), axis=1, keepdims=True)
    second = jnp.sum(jnp.where(held & (lane != first), 1, 0), axis=0, keepdims=True)
    tile_v[0:1, :] = as_row(jnp.minimum(first, TILES - 1))
    tile_v[1:2, :] = as_row(jnp.maximum(last, 0))
    where_v[...] = owner * 2 + second
    where_copy = pltpu.make_async_copy(where_v, where_s, local.at[0])
    tile_copy = pltpu.make_async_copy(tile_v, tile_s, local.at[1])
    where_copy.start()
    tile_copy.start()
    pl.semaphore_wait(barrier, len(near) + len(far))

    mine = table.at[pl.ds(rank, 1)]
    for where in near:
        remote(mine, mine, table_send, table_recv, where).start()
    others = table.at[pl.ds(0, len(near))]
    remote(others, others, table_send, table_recv, near[0]).wait()
    block = table.at[pl.ds((x * 4 + y) * 8, 8)]
    for where in far:
        remote(block, block, block_send, block_recv, where).start()
    others = table.at[pl.ds(0, len(far) * 8)]
    remote(others, others, block_send, block_recv, far[0]).wait()

    asked = table[...].reshape(128, 128)
    hit = (asked >> 5) == me
    key = lane * SLOTS + (asked & (SLOTS - 1))
    first = jnp.min(jnp.where(hit, key, TILES * SLOTS), axis=1, keepdims=True)
    last = jnp.max(jnp.where(hit, key, -1), axis=1, keepdims=True)
    chosen = (
        as_row(jnp.where(first < TILES * SLOTS, first & (SLOTS - 1), -1)),
        as_row(jnp.where(last > first, last & (SLOTS - 1), -1)),
    )
    for s in range(2):
        index_v[s:s + 1, :] = jnp.maximum(chosen[s], 0)
    cell = lax.broadcasted_iota(I32, (SLOTS, 128), 0)
    selector = jnp.concatenate([(cell == c).astype(F32).astype(BF16) for c in chosen], axis=1)
    index_copy = pltpu.make_async_copy(index_v, index_s, local.at[2])
    index_copy.start()

    def everyone(source, index, by_rank, landing, place, send, recv):
        for i, step in enumerate(STEPS):
            where, to_rank = device(step)
            peer = to_rank if by_rank else where[0] * col_count + where[1]
            for s in range(2):
                outgoing[2 * i + s] = source[index[s, peer]]
            remote(
                outgoing.at[pl.ds(2 * i, 2)], landing.at[pl.ds(2 * place, 2)], send, recv, where
            ).start()
        for s in range(2):
            landing[2 * place + s] = source[index[s, rank if by_rank else me]]

    def everyone_wait(landing, send, recv):
        others = pl.ds(0, 2 * (total - 1))
        remote(outgoing.at[others], landing.at[others], send, recv, near[0]).wait()

    index_copy.wait()
    everyone(cells3, index_s, True, arrived, me, cell_send, cell_recv)
    where_copy.wait()
    tile_copy.wait()
    target_copy.wait()
    build_bands(row_taps, col_taps, a_own, a_halo, at_own, at_rim, b_both, bt_both, taps_pad)
    for ref in (p_hi, p_lo):
        for k in range(KERNELS):
            ref[k, 0] = jnp.zeros((128, 128), BF16)
            ref[k, 9] = jnp.zeros((128, 128), BF16)
    for ref in (z_hi, z_lo):
        for parity in range(2):
            ref[parity, 0] = jnp.zeros((64, 128), BF16)
            ref[parity, 9] = jnp.zeros((64, 128), BF16)
    everyone_wait(arrived, cell_send, cell_recv)

    def put(t, carry):
        wide[1 + t // TILE_COLS, 1 + lax.rem(t, TILE_COLS)] = arrived[where_s[0, t]]
        return carry
    lax.fori_loop(0, TILES, put, 0, unroll=8)

    def halo(i, dr, dc):
        return remote(
            wide.at[span(dr, TILE_ROWS, True), span(dc, TILE_COLS, True)],
            wide.at[span(-dr, TILE_ROWS, False), span(-dc, TILE_COLS, False)],
            halo_send.at[i], halo_recv.at[i], (row + dr, col + dc),
        )
    start_copies(halo, at, counts, ACROSS + ALONG)
    rows_own(wide, a_own, x_own, x_low, early)
    wait_copies(halo, at, counts)

    forward(weight, wide, a_own, a_halo, b_both, x_own, x_low, x_halo, early, y_hi, y_lo, fields, power)
    products(weight, target, fields, power, p_hi, p_lo)

    def rim(i, dr, dc):
        side_row, side_col = int(dr > 0), 0 if dc < 0 else TILE_COLS + 1
        if dr == 0:
            source, landing = rim_col.at[int(dc > 0)], halo_col.at[int(dc > 0)]
        elif dc == 0:
            source, landing = rim_row.at[side_row, pl.ds(1, TILE_COLS)], halo_row.at[side_row]
        else:
            source, landing = rim_row.at[side_row, side_col], halo_corner.at[2 * side_row + int(dc > 0)]
        return remote(source, landing, rim_send.at[i], rim_recv.at[i], (row + dr, col + dc))

    for c, tiles in adjoint_rim(at_rim, bt_both, p_hi, p_lo, z_hi, z_lo):
        rim_row[:, c] = tiles
    start_copies(rim, at, counts, ACROSS)

    def keep_own(g, count):
        for c, tiles in adjoint_rows(at_own, g, count, q_hi, q_lo):
            if c in (0, TILE_COLS + 1):
                rim_col[int(c > 0)] = tiles
            elif c <= TILE_COLS:
                for a in range(TILE_ROWS):
                    own[TILE_COLS * a + c - 1] = tiles[a]
    adjoint_columns(bt_both, p_hi, p_lo, q_hi, q_lo, ((0, 1), (8, 1)))
    keep_own(0, 1)
    keep_own(8, 1)
    start_copies(rim, at, counts, ALONG)
    adjoint_columns(bt_both, p_hi, p_lo, q_hi, q_lo, ((1, 7),))
    for g, count in ((1, 2), (3, 2), (5, 2), (7, 1)):
        keep_own(g, count)
    wait_copies(rim, at, counts)
    own[96:128] = own[96:128] + halo_row[0]
    own[0:32] = own[0:32] + halo_row[1]
    for a in range(TILE_ROWS):
        t = TILE_COLS * a
        own[t + 31] = own[t + 31] + halo_col[0, a]
        own[t] = own[t] + halo_col[1, a]
    for i, t in enumerate((127, 96, 31, 0)):
        own[t] = own[t] + halo_corner[i]

    everyone(own, tile_s, False, back, rank, grad_send, grad_recv)
    everyone_wait(back, grad_send, grad_recv)
    flat = back.reshape(2 * TILES * 8, 128)
    for r in range(8):
        value = jnp.concatenate(
            [flat[pl.ds(8 * s + r, 128, stride=16), :] for s in range(2)], axis=0
        )
        high, low = split(value)
        tail = (value - high.astype(F32) - low.astype(F32)).astype(BF16)
        parts = mm(selector, jnp.concatenate([high, low, tail], axis=1))
        total_r = parts[:, 0:128] + parts[:, 128:256] + parts[:, 256:384]
        lanes = slice(128 * r, 128 * r + 128)
        out[:, lanes] = cells[:, lanes] - STEP_RATE * total_r


def shards(counts, cells, instance_cell, target, row_taps, col_taps, kernel_weight):
    vmem = pltpu.VMEM
    smem = pltpu.SMEM
    dma = pltpu.SemaphoreType.DMA
    return pl.pallas_call(
        functools.partial(step_kernel, counts),
        name="gradient_step",
        out_shape=jax.ShapeDtypeStruct((SLOTS, 1024), F32),
        in_specs=[SCALARS] + [WHOLE] * 4 + [pl.BlockSpec(memory_space=pl.ANY)],
        out_specs=WHOLE,
        scratch_shapes=[
            vmem((8, 128), I32), vmem((128, 1, 128), I32),
            vmem((SLOTS, 8, 128), F32), vmem((256, 8, 128), F32), vmem((256, 8, 128), F32),
            vmem((2, 128), I32), smem((2, 128), I32), vmem((1, 128), I32), smem((1, 128), I32),
            vmem((2, 128), I32), smem((2, 128), I32), vmem((6, WIDE, 8, 128), F32), vmem((ROWS, COLS), F32),
            vmem((1024, 256), BF16), vmem((1024, 256), BF16), vmem((256, 1024), BF16), vmem((8, 128, 256), BF16),
            vmem((8, 256, 256), BF16), vmem((8, 256, 256), BF16), vmem((16, 256), F32),
            vmem((256, 1152), BF16), vmem((128, 1152), BF16), vmem((256, 1152), BF16),
            vmem((3, 1024, 256), F32),
            vmem((8, 9, 128, 128), BF16), vmem((8, 9, 128, 128), BF16),
            vmem((8, 1024, 128), F32), vmem((1024, 128), F32),
            vmem((8, 10, 128, 128), BF16), vmem((8, 10, 128, 128), BF16),
            vmem((2, 10, 64, 128), BF16), vmem((2, 10, 64, 128), BF16),
            vmem((1024, 1152), BF16), vmem((1024, 1152), BF16),
            vmem((2, WIDE, 8, 128), F32), vmem((2, 4, 8, 128), F32),
            vmem((2, 32, 8, 128), F32), vmem((2, 4, 8, 128), F32), vmem((4, 8, 128), F32),
            vmem((TILES, 8, 128), F32), vmem((256, 8, 128), F32),
        ] + [dma] * 8 + [dma((8,))] * 4 + [dma((4,))],
        compiler_params=pltpu.CompilerParams(collective_id=0, has_side_effects=True),
    )(kernel_weight, instance_cell, cells, row_taps, col_taps, target)


def solution(mesh):
    placed = (P(("row", "col"), None), P("row", "col"), P("row", "col"), P(), P(), P())
    return jax.shard_map(
        functools.partial(shards, (mesh.shape["row"], mesh.shape["col"])),
        mesh=mesh, in_specs=placed, out_specs=P(("row", "col"), None), check_vma=False,
    )
```

```python
import functools
import itertools

import jax
import jax.numpy as jnp
from jax import lax
from jax.experimental import pallas as pl
from jax.experimental.pallas import tpu as pltpu
from jax.sharding import PartitionSpec as P

TILE = 32
TAPS = 65
KERNELS = 8
ROWS = 128
COLS = 1024
TILE_ROWS = 4
TILE_COLS = 32
TILES = 128
SLOTS = 32
WIDE = 36
GROUPS = 9
STEEPNESS = 4.0
THRESHOLD = 0.3
STEP_RATE = 0.5
MESH = pl.DeviceIdType.MESH
BF16 = jnp.bfloat16
F32 = jnp.float32
I32 = jnp.int32
WHOLE = pl.BlockSpec(memory_space=pltpu.VMEM)
SCALARS = pl.BlockSpec(memory_space=pltpu.SMEM)

NEIGHBOURS = tuple((dr, dc) for dr in (-1, 0, 1) for dc in (-1, 0, 1) if (dr, dc) != (0, 0))


def span(step, count, inside):
    if step == 0:
        return pl.ds(1, count)
    if step < 0:
        return pl.ds(1 if inside else 0, 1)
    return pl.ds(count if inside else count + 1, 1)


def split(value):
    high = value.astype(BF16)
    return high, (value - high.astype(F32)).astype(BF16)


def mm(a, b):
    return jnp.dot(a, b, preferred_element_type=F32)


def swap_blocks(vectors):
    lane = lax.broadcasted_iota(I32, vectors[0].shape, 2)
    low = lane < 64
    even = (lane & 32) == 0
    a, b, c, d = vectors
    a, c = (
        jnp.where(low, a, pltpu.roll(c, 64, 2)),
        jnp.where(low, pltpu.roll(a, 64, 2), c),
    )
    b, d = (
        jnp.where(low, b, pltpu.roll(d, 64, 2)),
        jnp.where(low, pltpu.roll(b, 64, 2), d),
    )
    a, b = (
        jnp.where(even, a, pltpu.roll(b, 32, 2)),
        jnp.where(even, pltpu.roll(a, 96, 2), b),
    )
    c, d = (
        jnp.where(even, c, pltpu.roll(d, 32, 2)),
        jnp.where(even, pltpu.roll(c, 96, 2), d),
    )
    return a, b, c, d


def lanes_of(g, count=1):
    return pl.ds(g * 128, 128 * count)


def build_bands(weight, row_taps, col_taps, a_own, a_halo, at_own, at_rim, b_both, bt_both, pad):
    pad[...] = jnp.zeros_like(pad)
    pad[0:8, 0:TAPS] = row_taps[...]
    pad[8:16, 0:TAPS] = col_taps[...]
    c = lax.broadcasted_iota(I32, (256, 256), 0)
    p = lax.broadcasted_iota(I32, (256, 256), 1)
    inner = ((c & 3) << 3) + ((c & 31) >> 2)
    tile = c >> 5
    is_own = (tile >= 1) & (tile <= 4)
    own_at = jnp.where(is_own, 32 * tile - 32 + inner, -1024)
    halo_at = jnp.where(tile == 0, inner, jnp.where(tile == 5, 32 + inner, -1024))

    def ones(condition):
        return condition.astype(F32).astype(BF16)
    own_high, own_low = ones(p == own_at), ones(p == own_at + 128)
    halo_high, halo_low = ones((p == halo_at) | (p == halo_at + 128)), ones(p == halo_at + 64)

    def shifted(line):
        row = pad[pl.ds(line, 1), :]
        return pltpu.roll(jnp.broadcast_to(row, (128, 256)), 0, 1, stride=1, stride_axis=0)

    for k in range(KERNELS):
        rows = pl.ds(k * 128, 128)
        high, low = split(shifted(k))
        own = mm(high, own_high) + mm(low, own_low)
        halo = mm(high, halo_high) + mm(low, halo_low)
        a_own[rows, :] = own.astype(BF16)
        a_halo[rows, :] = halo.astype(BF16)
        at_own[:, rows] = own.T.astype(BF16)
        turned = halo.T
        for h in range(2):
            at_rim[k, :, 128 * h:128 * h + 128] = turned[0:128].astype(BF16)
        root = jnp.sqrt(jnp.full((1, 256), weight[k], F32))
        band = shifted(8 + k) * root
        for i, part in enumerate(split(band)):
            b_both[k, :, lanes_of(i)] = part.astype(F32).T.astype(BF16)
        for i, part in enumerate(split(band * (4.0 * STEEPNESS))):
            bt_both[k, 0:128, lanes_of(i)] = part[:, 128:256]
            bt_both[k, 128:256, lanes_of(i)] = part[:, 0:128]


EARLY = (1, 3, 5)


def mask_own(g, wide, x_own, x_low):
    turned = swap_blocks([wide[1:5, 4 * g + q] for q in range(4)])
    high, low = split(jnp.concatenate(turned, axis=1).reshape(128, 128))
    x_own[0:128, lanes_of(g)] = high
    x_own[128:256, lanes_of(g)] = high
    x_low[:, lanes_of(g)] = low


def rows_own(wide, a_own, x_own, x_low, early):
    for i, g in enumerate(EARLY):
        for h in (g, g + 1):
            mask_own(h, wide, x_own, x_low)
        lanes = lanes_of(g, 2)
        early[i] = mm(a_own[...], x_own[:, lanes]) + mm(a_own[:, 0:128], x_low[:, lanes])
    mask_own(7, wide, x_own, x_low)


def forward_rows(wide, a_own, a_halo, x_own, x_low, x_halo, early, y_hi, y_lo):
    for g in (0, 8):
        mask_own(g, wide, x_own, x_low)
    x_halo[192:256, :] = jnp.zeros((64, GROUPS * 128), BF16)
    for g in range(GROUPS):
        sides = [jnp.stack([wide[0, 4 * g + q], wide[5, 4 * g + q]]) for q in range(4)]
        value = jnp.concatenate(swap_blocks(sides), axis=1).reshape(64, 128)
        high, low = split(value)
        lanes = lanes_of(g)
        x_halo[0:64, lanes] = high
        x_halo[64:128, lanes] = high
        x_halo[128:192, lanes] = low

    def keep(g, value):
        y_hi[:, g], y_lo[:, g] = (v.reshape(KERNELS, 128, 128) for v in split(value))
    lanes = lanes_of(7, 2)
    value = (
        mm(a_own[...], x_own[:, lanes]) + mm(a_own[:, 0:128], x_low[:, lanes]) + mm(a_halo[...], x_halo[:, lanes])
    )
    for h in range(2):
        keep(7 + h, value[:, 128 * h:128 * h + 128])
    lanes = lanes_of(0)
    beside = jnp.concatenate([x_low[:, lanes], jnp.zeros((128, 128), BF16)], axis=0)
    both = mm(a_own[...], jnp.concatenate([x_own[:, lanes], beside], axis=1))
    keep(0, both[:, 0:128] + both[:, 128:256] + mm(a_halo[...], x_halo[:, lanes]))
    for i, g in enumerate(EARLY):
        value = early[i] + mm(a_halo[...], x_halo[:, lanes_of(g, 2)])
        for h in range(2):
            keep(g + h, value[:, 128 * h:128 * h + 128])


def image(target, b_both, y_hi, y_lo, fields, p_hi, p_lo):
    for n in range(0, 8, 2):
        part = pl.ds(128 * n, 256)
        intensity = None
        for k in range(KERNELS):
            both = mm(windows(y_hi.at[k], n, 2), b_both[k])
            field = both[:, :128] + both[:, 128:] + mm(windows(y_lo.at[k], n, 2), b_both[k, :, 0:128])
            fields[k, part] = field
            intensity = field * field if k == 0 else intensity + field * field
        wanted = jnp.concatenate([target[:, lanes_of(n)], target[:, lanes_of(n + 1)]], axis=0)
        resist = 1.0 / (1.0 + jnp.exp(-STEEPNESS * (intensity - THRESHOLD)))
        sensitivity = (resist - wanted) * resist * (1.0 - resist)
        for k in range(KERNELS):
            parts = split(sensitivity * fields[k, part])
            p_hi[k, n + 1:n + 3], p_lo[k, n + 1:n + 3] = (v.reshape(2, 128, 128) for v in parts)


def windows(ref, start, count):
    rows = count * ref.shape[1]
    return jnp.concatenate(
        [ref[start:start + count].reshape(rows, 128), ref[start + 1:start + 1 + count].reshape(rows, 128)], axis=1
    )


def adjoint_rim(at_rim, bt_both, p_hi, p_lo, z_hi, z_lo):
    total = jnp.zeros((64 * GROUPS, 128), F32)
    for k in range(KERNELS):
        high, low = z_hi.at[k % 2], z_lo.at[k % 2]
        for n in (1, 3, 5, 7):
            upper = jnp.concatenate([p_hi[k, n], p_hi[k, n + 1]], axis=1)
            lower = jnp.concatenate([p_lo[k, n], p_lo[k, n + 1]], axis=1)
            both = mm(at_rim[k], jnp.concatenate([upper, lower], axis=0))
            value = both[0:64] + both[64:128]
            for h in range(2):
                high[n + h], low[n + h] = split(value[:, 128 * h:128 * h + 128])
        both = mm(windows(high, 0, GROUPS), bt_both[k])
        total = total + both[:, :128] + both[:, 128:] + mm(windows(low, 0, GROUPS), bt_both[k, :, 0:128])
    tiles = []
    for g in range(GROUPS):
        tiles += as_tiles(total[64 * g:64 * g + 64], g)
    return tiles


def as_tiles(value, g):
    value = value.reshape(value.shape[0] // 32, 32, 128)
    turned = swap_blocks([value[:, 8 * s:8 * s + 8] for s in range(4)])
    return [(4 * g + q, turned[q]) for q in range(4)]


def adjoint_columns(bt_both, p_hi, p_lo, q_hi, q_lo, groups):
    for k in range(KERNELS):
        def window(ref):
            return jnp.concatenate([windows(ref.at[k], start, count) for start, count in groups], axis=0)
        both = mm(window(p_hi), bt_both[k])
        value = both[:, :128] + both[:, 128:] + mm(window(p_lo), bt_both[k, :, 0:128])
        high, low = split(value)
        rows = pl.ds(k * 128, 128)
        for i, g in enumerate(g for start, count in groups for g in range(start, start + count)):
            q_hi[rows, lanes_of(g)] = high[128 * i:128 * i + 128]
            q_lo[rows, lanes_of(g)] = low[128 * i:128 * i + 128]


def adjoint_rows(bands, g, count, q_hi, q_lo):
    lanes = lanes_of(g, count)
    if count == 1:
        both = mm(bands[...], jnp.concatenate([q_hi[:, lanes], q_lo[:, lanes]], axis=1))
        both = both[:, 0:128] + both[:, 128:256]
        return as_tiles(both[0:128] + both[128:256], g)
    both = mm(bands[...], q_hi[:, lanes])
    value = both[0:128] + both[128:256] + mm(bands[0:128, :], q_lo[:, lanes])
    return as_tiles(value[:, 0:128], g) + as_tiles(value[:, 128:256], g + 1)


def exists(at, counts, step):
    ok = None
    for a, count, d in zip(at, counts, step):
        if d:
            here = (a + d >= 0) if d < 0 else (a + d < count)
            ok = here if ok is None else jnp.logical_and(ok, here)
    return ok


def start_copies(copy, at, counts, which):
    for i in which:
        @pl.when(exists(at, counts, NEIGHBOURS[i]))
        def _():
            copy(i, *NEIGHBOURS[i]).start()


def wait_copies(copy, at, counts):
    for i, (dr, dc) in enumerate(NEIGHBOURS):
        @pl.when(exists(at, counts, (dr, dc)))
        def _():
            copy(i, dr, dc).wait_send()

        @pl.when(exists(at, counts, (-dr, -dc)))
        def _():
            copy(i, dr, dc).wait_recv()


ACROSS = sorted((i for i, (dr, dc) in enumerate(NEIGHBOURS) if dr), key=lambda i: NEIGHBOURS[i][1] == 0)
ALONG = [i for i, (dr, dc) in enumerate(NEIGHBOURS) if not dr]


def hops(step):
    return sum(min(d, 4 - d) for d in step[:3])


STEPS = sorted((s for s in itertools.product(range(4), range(4), range(4), range(2)) if any(s)), key=lambda s: -hops(s))


def step_kernel(
    counts, weight, inst, cells, row_taps, col_taps, target_hbm, out,
    pad, table, cells3, outgoing, arrived, index_v, index_s, where_v, where_s, tile_v, tile_s, wide, target,
    a_own, a_halo, at_own, at_rim, b_both, bt_both, taps_pad,
    x_own, x_low, x_halo, early, y_hi, y_lo, fields, p_hi, p_lo, z_hi, z_lo, q_hi, q_lo,
    rim_row, rim_col, halo_row, halo_col, halo_corner, own, back,
    table_send, table_recv, block_send, block_recv, cell_send, cell_recv, grad_send, grad_recv,
    halo_send, halo_recv, rim_send, rim_recv, local,
):
    row_count, col_count = counts
    total = row_count * col_count
    at = row, col = lax.axis_index("row"), lax.axis_index("col")
    me = row * col_count + col
    barrier = pltpu.get_barrier_semaphore()
    core, z = lax.rem(row, 2), lax.rem(row // 2, 4)
    y, x = (row // 8) * 2 + lax.rem(col, 2), col // 2

    def device(step):
        dx, dy, dz, dcore = step
        to = lax.rem(x + dx, 4), lax.rem(y + dy, 4), lax.rem(z + dz, 4), lax.rem(core + dcore, 2)
        where = (to[1] // 2) * 8 + to[2] * 2 + to[3], to[0] * 2 + lax.rem(to[1], 2)
        return where, ((to[0] * 4 + to[1]) * 4 + to[2]) * 2 + to[3]
    rank = ((x * 4 + y) * 4 + z) * 2 + core
    near = [device(s)[0] for s in STEPS if s[0] == s[1] == 0]
    far = [device(s)[0] for s in STEPS if s[2] == s[3] == 0]

    def remote(source, landing, send, recv, where):
        return pltpu.make_async_remote_copy(
            src_ref=source, dst_ref=landing, send_sem=send, recv_sem=recv,
            device_id=where, device_id_type=MESH,
        )

    for a in (0, 5):
        wide[a] = jnp.zeros((WIDE, 8, 128), F32)
    for b in (0, 33, 34, 35):
        wide[1:5, b] = jnp.zeros((TILE_ROWS, 8, 128), F32)
    for ref in (halo_row, halo_col, halo_corner):
        ref[...] = jnp.zeros_like(ref)
    for where in far + near:
        pl.semaphore_signal(barrier, inc=1, device_id=where, device_id_type=MESH)
    target_copy = pltpu.make_async_copy(target_hbm, target, local.at[3])
    target_copy.start()
    pad[...] = jnp.zeros_like(pad)
    pad[0:TILE_ROWS, 0:TILE_COLS] = inst[...]
    lines = pad[...]
    line = lax.broadcasted_iota(I32, lines.shape, 0)
    flat = jnp.zeros((8, 128), I32)
    for a in range(TILE_ROWS):
        moved = pltpu.roll(lines, 32 * a, 1) if a else lines
        flat = flat + jnp.where(line == a, moved, 0)
    flat = jnp.sum(flat, axis=0, keepdims=True)
    table[rank] = flat
    for r in range(8):
        cells3[:, r, :] = cells[:, 128 * r:128 * r + 128]
    lane = lax.broadcasted_iota(I32, (128, 128), 1)
    sub = lax.broadcasted_iota(I32, (128, 128), 0)
    diagonal = lane == sub

    def as_row(column):
        return jnp.sum(jnp.where(diagonal, column, 0), axis=0, keepdims=True)
    owner = flat >> 5
    held = owner == sub
    first = jnp.min(jnp.where(held, lane, TILES), axis=1, keepdims=True)
    last = jnp.max(jnp.where(held, lane, -1), axis=1, keepdims=True)
    second = jnp.sum(jnp.where(held & (lane != first), 1, 0), axis=0, keepdims=True)
    tile_v[0:1, :] = as_row(jnp.minimum(first, TILES - 1))
    tile_v[1:2, :] = as_row(jnp.maximum(last, 0))
    where_v[...] = owner * 2 + second
    where_copy = pltpu.make_async_copy(where_v, where_s, local.at[0])
    tile_copy = pltpu.make_async_copy(tile_v, tile_s, local.at[1])
    where_copy.start()
    tile_copy.start()
    pl.semaphore_wait(barrier, len(near) + len(far))

    mine = table.at[pl.ds(rank, 1)]
    for where in near:
        remote(mine, mine, table_send, table_recv, where).start()
    others = table.at[pl.ds(0, len(near))]
    remote(others, others, table_send, table_recv, near[0]).wait()
    block = table.at[pl.ds((x * 4 + y) * 8, 8)]
    for where in far:
        remote(block, block, block_send, block_recv, where).start()
    others = table.at[pl.ds(0, len(far) * 8)]
    remote(others, others, block_send, block_recv, far[0]).wait()

    asked = table[...].reshape(128, 128)
    hit = (asked >> 5) == me
    key = lane * SLOTS + (asked & (SLOTS - 1))
    first = jnp.min(jnp.where(hit, key, TILES * SLOTS), axis=1, keepdims=True)
    last = jnp.max(jnp.where(hit, key, -1), axis=1, keepdims=True)
    chosen = (
        as_row(jnp.where(first < TILES * SLOTS, first & (SLOTS - 1), -1)),
        as_row(jnp.where(last > first, last & (SLOTS - 1), -1)),
    )
    for s in range(2):
        index_v[s:s + 1, :] = jnp.maximum(chosen[s], 0)
    cell = lax.broadcasted_iota(I32, (SLOTS, 128), 0)
    selector = jnp.concatenate([(cell == c).astype(F32).astype(BF16) for c in chosen], axis=1)
    index_copy = pltpu.make_async_copy(index_v, index_s, local.at[2])
    index_copy.start()

    def everyone(source, index, by_rank, landing, place, send, recv):
        for i, step in enumerate(STEPS):
            where, to_rank = device(step)
            peer = to_rank if by_rank else where[0] * col_count + where[1]
            for s in range(2):
                outgoing[2 * i + s] = source[index[s, peer]]
            remote(
                outgoing.at[pl.ds(2 * i, 2)], landing.at[pl.ds(2 * place, 2)], send, recv, where
            ).start()
        for s in range(2):
            landing[2 * place + s] = source[index[s, rank if by_rank else me]]

    def everyone_wait(landing, send, recv):
        others = pl.ds(0, 2 * (total - 1))
        remote(outgoing.at[others], landing.at[others], send, recv, near[0]).wait()

    index_copy.wait()
    everyone(cells3, index_s, True, arrived, me, cell_send, cell_recv)
    where_copy.wait()
    tile_copy.wait()
    target_copy.wait()
    build_bands(weight, row_taps, col_taps, a_own, a_halo, at_own, at_rim, b_both, bt_both, taps_pad)
    for ref in (p_hi, p_lo):
        for k in range(KERNELS):
            ref[k, 0] = jnp.zeros((128, 128), BF16)
            ref[k, 9] = jnp.zeros((128, 128), BF16)
    for ref in (z_hi, z_lo):
        for parity in range(2):
            ref[parity, 0] = jnp.zeros((64, 128), BF16)
            ref[parity, 9] = jnp.zeros((64, 128), BF16)
    everyone_wait(arrived, cell_send, cell_recv)

    def put(t, carry):
        wide[1 + t // TILE_COLS, 1 + lax.rem(t, TILE_COLS)] = arrived[where_s[0, t]]
        return carry
    lax.fori_loop(0, TILES, put, 0, unroll=8)

    def halo(i, dr, dc):
        return remote(
            wide.at[span(dr, TILE_ROWS, True), span(dc, TILE_COLS, True)],
            wide.at[span(-dr, TILE_ROWS, False), span(-dc, TILE_COLS, False)],
            halo_send.at[i], halo_recv.at[i], (row + dr, col + dc),
        )
    start_copies(halo, at, counts, ACROSS + ALONG)
    rows_own(wide, a_own, x_own, x_low, early)
    wait_copies(halo, at, counts)

    forward_rows(wide, a_own, a_halo, x_own, x_low, x_halo, early, y_hi, y_lo)
    image(target, b_both, y_hi, y_lo, fields, p_hi, p_lo)

    def rim(i, dr, dc):
        side_row, side_col = int(dr > 0), 0 if dc < 0 else TILE_COLS + 1
        if dr == 0:
            source, landing = rim_col.at[int(dc > 0)], halo_col.at[int(dc > 0)]
        elif dc == 0:
            source, landing = rim_row.at[side_row, pl.ds(1, TILE_COLS)], halo_row.at[side_row]
        else:
            source, landing = rim_row.at[side_row, side_col], halo_corner.at[2 * side_row + int(dc > 0)]
        return remote(source, landing, rim_send.at[i], rim_recv.at[i], (row + dr, col + dc))

    for c, tiles in adjoint_rim(at_rim, bt_both, p_hi, p_lo, z_hi, z_lo):
        rim_row[:, c] = tiles
    start_copies(rim, at, counts, ACROSS)

    def keep_own(g, count):
        for c, tiles in adjoint_rows(at_own, g, count, q_hi, q_lo):
            if c in (0, TILE_COLS + 1):
                rim_col[int(c > 0)] = tiles
            elif c <= TILE_COLS:
                for a in range(TILE_ROWS):
                    own[TILE_COLS * a + c - 1] = tiles[a]
    adjoint_columns(bt_both, p_hi, p_lo, q_hi, q_lo, ((0, 1), (8, 1)))
    keep_own(0, 1)
    keep_own(8, 1)
    start_copies(rim, at, counts, ALONG)
    adjoint_columns(bt_both, p_hi, p_lo, q_hi, q_lo, ((1, 7),))
    for g, count in ((1, 2), (3, 2), (5, 2), (7, 1)):
        keep_own(g, count)
    wait_copies(rim, at, counts)
    own[96:128] = own[96:128] + halo_row[0]
    own[0:32] = own[0:32] + halo_row[1]
    for a in range(TILE_ROWS):
        t = TILE_COLS * a
        own[t + 31] = own[t + 31] + halo_col[0, a]
        own[t] = own[t] + halo_col[1, a]
    for i, t in enumerate((127, 96, 31, 0)):
        own[t] = own[t] + halo_corner[i]

    everyone(own, tile_s, False, back, rank, grad_send, grad_recv)
    everyone_wait(back, grad_send, grad_recv)
    flat = back.reshape(2 * TILES * 8, 128)
    for r in range(8):
        value = jnp.concatenate(
            [flat[pl.ds(8 * s + r, 128, stride=16), :] for s in range(2)], axis=0
        )
        high, low = split(value)
        tail = (value - high.astype(F32) - low.astype(F32)).astype(BF16)
        parts = mm(selector, jnp.concatenate([high, low, tail], axis=1))
        total_r = parts[:, 0:128] + parts[:, 128:256] + parts[:, 256:384]
        lanes = slice(128 * r, 128 * r + 128)
        out[:, lanes] = cells[:, lanes] - STEP_RATE * total_r


def shards(counts, cells, instance_cell, target, row_taps, col_taps, kernel_weight):
    vmem = pltpu.VMEM
    smem = pltpu.SMEM
    dma = pltpu.SemaphoreType.DMA
    return pl.pallas_call(
        functools.partial(step_kernel, counts),
        name="gradient_step",
        out_shape=jax.ShapeDtypeStruct((SLOTS, 1024), F32),
        in_specs=[SCALARS] + [WHOLE] * 4 + [pl.BlockSpec(memory_space=pl.ANY)],
        out_specs=WHOLE,
        scratch_shapes=[
            vmem((8, 128), I32), vmem((128, 1, 128), I32),
            vmem((SLOTS, 8, 128), F32), vmem((256, 8, 128), F32), vmem((256, 8, 128), F32),
            vmem((2, 128), I32), smem((2, 128), I32), vmem((1, 128), I32), smem((1, 128), I32),
            vmem((2, 128), I32), smem((2, 128), I32), vmem((6, WIDE, 8, 128), F32), vmem((ROWS, COLS), F32),
            vmem((1024, 256), BF16), vmem((1024, 256), BF16), vmem((256, 1024), BF16), vmem((8, 128, 256), BF16),
            vmem((8, 256, 256), BF16), vmem((8, 256, 256), BF16), vmem((16, 256), F32),
            vmem((256, 1152), BF16), vmem((128, 1152), BF16), vmem((256, 1152), BF16),
            vmem((3, 1024, 256), F32),
            vmem((8, 9, 128, 128), BF16), vmem((8, 9, 128, 128), BF16),
            vmem((8, 1024, 128), F32),
            vmem((8, 10, 128, 128), BF16), vmem((8, 10, 128, 128), BF16),
            vmem((2, 10, 64, 128), BF16), vmem((2, 10, 64, 128), BF16),
            vmem((1024, 1152), BF16), vmem((1024, 1152), BF16),
            vmem((2, WIDE, 8, 128), F32), vmem((2, 4, 8, 128), F32),
            vmem((2, 32, 8, 128), F32), vmem((2, 4, 8, 128), F32), vmem((4, 8, 128), F32),
            vmem((TILES, 8, 128), F32), vmem((256, 8, 128), F32),
        ] + [dma] * 8 + [dma((8,))] * 4 + [dma((4,))],
        compiler_params=pltpu.CompilerParams(collective_id=0, has_side_effects=True),
    )(kernel_weight, instance_cell, cells, row_taps, col_taps, target)


def solution(mesh):
    placed = (P(("row", "col"), None), P("row", "col"), P("row", "col"), P(), P(), P())
    return jax.shard_map(
        functools.partial(shards, (mesh.shape["row"], mesh.shape["col"])),
        mesh=mesh, in_specs=placed, out_specs=P(("row", "col"), None), check_vma=False,
    )
```
